128 devices in a mesh: pool: 32 (over y, x, core), grp: 4 (over z).
Axes of the slice: x: 4, y: 4, z: 4, core: 2. Of those that a mesh axis runs over, the one named last changes fastest.
Arguments:
- mel_rows: bfloat16 [4096, 1920], P(('grp', 'pool')), parts along dimension 0, may hold values from -6 to 6
- old_cache: bfloat16 [8192, 6656], P(('grp', 'pool')), parts along dimension 0, may hold values from -6 to 6
- new_owner: int32 [4096, 1], P('grp'), parts along dimension 0, may hold values from 0 to 31; in each aligned block of 32 rows (0 to 31, 32 to 63, ...) at most 2 rows name the same one
- prev_owner: int32 [4096, 1], P('grp'), parts along dimension 0, may hold values from 0 to 31; in each aligned block of 32 rows (0 to 31, 32 to 63, ...) at most 2 rows name the same one
- active: int32 [4096], P('grp'), parts along dimension 0, may hold values 0 or 1
- w_pre: bfloat16 [560, 512], replicated, may hold values from -0.25 to 0.25
- w_up: bfloat16 [1024, 2048], replicated, may hold values from -0.1875 to 0.1875
- res_first: bfloat16 [3, 768, 256], replicated, may hold values from -0.21875 to 0.21875
- res_second: bfloat16 [3, 768, 256], replicated, may hold values from -0.21875 to 0.21875
Outputs:
- wave_features: bfloat16 [4096, 36864], P(('grp', 'pool')), parts along dimension 0
- new_cache: bfloat16 [8192, 6656], P(('grp', 'pool')), parts along dimension 0
The draws below stay inside these ranges and needn't reach their ends.
There are 4 independent parts, one for each index of `grp`. The reference program is written for one: setup_inputs(seed, part) draws one part's arguments, and reference() takes and returns one part's arrays. A program takes and returns all parts, laid end to end along the dimension named above; an argument that names none is the same for every part. Nothing has to cross between parts.
Inputs may be any that keep to these rules, and one draw needn't show every extreme that they name: `new_owner`: among the 32 utterances of one home no owner is named more than 2 times, a bound that some block reaches. `prev_owner`: among the 32 utterances of one home no owner is named more than 2 times, a bound that some block reaches.
All inputs are finite; a program needn't handle non-finite values.
Results may differ from the reference program's by a relative error of at most 0.0058.
Values may be sent and summed in bfloat16 or wider, within the bound.
A program may use at most 128 MiB of HBM per device.

```python
import math
import jax
import jax.numpy as jnp
import numpy as np
from jax import lax

C0 = 512
C1 = 256
MELS = 80
UP = 8
FRAMES = 18
LOOK = 6
U_DEV = 32
UTT = 1024
CAP = 2
SLOTS = 64
CACHE_W = 6656
N_POOL = 32


def with_ends(drawn, own_key, smallest, largest):
    dims = drawn.shape
    spot = [jax.random.randint(jax.random.fold_in(own_key, axis), (), 0, dims[axis]) for axis in range(len(dims))]
    drawn = drawn.at[tuple(spot)].set(smallest)
    longest = dims.index(max(dims))
    spot[longest] = (spot[longest] + 1) % dims[longest]
    return drawn.at[tuple(spot)].set(largest)


def shard_levels(stream_key, extent, split, low, largest):
    level, own = 1.0, jax.random.fold_in(stream_key, 6)
    for dim, shards_of in split:
        steps = jnp.exp(jax.random.uniform(jax.random.fold_in(own, dim), (shards_of,), jnp.float32, low / len(split), largest / len(split)))
        level = level * jnp.repeat(steps, extent[dim] // shards_of).reshape([-1 if axis == dim else 1 for axis in range(len(extent))])
    return level


def shared_out(key, own, number, rows, number_of, top, reach, lean):
    ranking = jax.random.permutation(key, number_of)
    packed, ordinary = load_shares(number_of, rows * top, reach, lean, True), load_shares(number_of, rows * top, reach, lean, False)
    places = jnp.arange(number_of)

    def named(tallies, rotation):
        used = int((tallies > 0).sum())
        fixed = max(1, used // 4)
        shifted = fixed + (places - fixed + rotation * (used - fixed)) % max(1, number_of - fixed)
        return jnp.zeros((number_of,), jnp.int32).at[ranking[jnp.where(places < fixed, places, shifted)]].set(jnp.asarray(tallies, jnp.int32))

    tallies = jnp.where(number % 4 == 0, named(packed, number // 4), named(ordinary, number - number // 4 - 1))
    mixed = jax.random.permutation(jax.random.fold_in(own, 3), number_of)
    giver, taker = mixed[0:number_of // 2 * 2:2], mixed[1:number_of // 2 * 2:2]
    margin = jnp.minimum(tallies[giver] - 1, reach - tallies[taker]) // 2
    margin = jnp.where((giver == ranking[0]) | (taker == ranking[0]) | (tallies[taker] == 0), 0, jnp.maximum(margin, 0))
    shifted = jax.random.randint(jax.random.fold_in(own, 4), (number_of // 2,), 0, 1 << 20) % (margin + 1)
    tallies = tallies.at[giver].add(-shifted).at[taker].add(shifted)
    labels = jnp.searchsorted(jnp.cumsum(tallies), jnp.arange(rows * top), side="right").astype(jnp.int32)
    grid = labels.reshape(top, rows).T
    grid = grid[jax.random.permutation(jax.random.fold_in(own, 1), rows)]
    rotation = jax.random.randint(jax.random.fold_in(own, 2), (rows, 1), 0, top)
    return jnp.take_along_axis(grid, (jnp.arange(top)[None, :] + rotation) % top, axis=1)


def load_shares(count, total, bound, skew, full):
    loads = [(1 << 20) // math.isqrt(grade ** skew) + 1 for grade in range(1, count + 1)]
    largest = bound if full else min(bound, max(-(-total // count), total * loads[0] // sum(loads)))
    least = 1 if total - largest >= count - 1 else 0
    given, rest = [largest] + [least] * (count - 1), total - largest - least * (count - 1)
    while rest > 0:
        free = [i for i in range(1, count) if given[i] < largest] or [i for i in range(1, count) if given[i] < bound]
        mass, budget = sum([loads[i] for i in free]), rest
        for i in free:
            more = min(bound - given[i], max(1, budget * loads[i] // mass), rest)
            given[i] = given[i] + more
            rest = rest - more
    return np.array(given)


def normal_values(own_key, shape, spread, reach, shards=(), held_as=jnp.bfloat16):
    entries = spread * jax.random.normal(own_key, shape, jnp.float32)
    if shards:
        entries = entries * shard_levels(own_key, shape, shards, -0.22, 0.18)
    return jnp.clip(entries, -reach, reach).astype(held_as)


def setup_inputs(seed: int = 0, part: int = 0) -> dict:
    key_of = jax.random.split(jax.random.key(seed), 10)
    part_keys = jax.random.split(jax.random.fold_in(key_of[9], part), 10)
    mel_rows = normal_values(part_keys[0], (UTT, (FRAMES + LOOK) * MELS), 1.0, 6.0, ((0, 32),))
    old_cache = normal_values(part_keys[1], (N_POOL * SLOTS, CACHE_W), 1.0, 6.0, ((0, 32),))
    new_owner_keys = jax.random.split(jax.random.fold_in(part_keys[2], 1), UTT // U_DEV)
    new_owner_turns = jax.random.permutation(jax.random.fold_in(part_keys[2], 3), UTT // U_DEV)
    new_owner = jax.vmap(lambda own, number: shared_out(jax.random.fold_in(part_keys[2], 2), own, number, U_DEV, N_POOL, 1, CAP, 2))(new_owner_keys, new_owner_turns).reshape((UTT, 1))
    prev_owner_keys = jax.random.split(jax.random.fold_in(part_keys[3], 1), UTT // U_DEV)
    prev_owner_turns = jax.random.permutation(jax.random.fold_in(part_keys[3], 3), UTT // U_DEV)
    prev_owner = jax.vmap(lambda own, number: shared_out(jax.random.fold_in(part_keys[3], 2), own, number, U_DEV, N_POOL, 1, CAP, 2))(prev_owner_keys, prev_owner_turns).reshape((UTT, 1))
    active = with_ends((jax.random.randint(part_keys[4], (UTT,), 0, 4) < 3).astype(jnp.int32), jax.random.fold_in(part_keys[4], 1), 0, 1)
    w_pre = normal_values(key_of[5], ((LOOK + 1) * MELS, C0), ((LOOK + 1) * MELS) ** -0.5, 0.25)
    w_up = normal_values(key_of[6], (2 * C0, UP * C1), (2 * C0) ** -0.5, 0.1875)
    res_first = normal_values(key_of[7], (3, 3 * C1, C1), (3 * C1) ** -0.5, 0.21875)
    res_second = normal_values(key_of[8], (3, 3 * C1, C1), (3 * C1) ** -0.5, 0.21875)
    return {"mel_rows": mel_rows, "old_cache": old_cache, "new_owner": new_owner, "prev_owner": prev_owner, "active": active, "w_pre": w_pre, "w_up": w_up, "res_first": res_first, "res_second": res_second}


DILATIONS = (1, 3, 5)
SLOPE = 0.1


def leaky_relu(values):
    return jnp.where(values >= 0, values, SLOPE * values)


def shifted_columns(sequence, dilation, length):
    return jnp.concatenate([sequence[:, tap_index * dilation: tap_index * dilation + length, :] for tap_index in range(3)], axis=-1)


def vocode(mel_block, caches, w_pre, w_up, res_first, res_second):
    rows_here = mel_block.shape[0]
    frames_in = mel_block.reshape(rows_here, FRAMES + LOOK, MELS)
    window = jnp.concatenate([frames_in[:, tap_index: tap_index + FRAMES, :] for tap_index in range(LOOK + 1)], axis=-1)
    window = window.reshape(rows_here * FRAMES, (LOOK + 1) * MELS)
    pre_out = jnp.dot(window, w_pre, preferred_element_type=jnp.float32).reshape(rows_here, FRAMES, C0)
    pre_last = caches[:, :C0].reshape(rows_here, 1, C0)
    up_input = jnp.concatenate([pre_last, leaky_relu(pre_out).astype(jnp.bfloat16)], axis=1)
    paired = jnp.concatenate([up_input[:, :-1], up_input[:, 1:]], axis=-1).reshape(rows_here * FRAMES, 2 * C0)
    length = UP * FRAMES
    stream = jnp.dot(paired, w_up, preferred_element_type=jnp.float32).reshape(rows_here, length, C1)
    kept_parts = [up_input[:, FRAMES]]
    offset = C0
    for section, dilation in enumerate(DILATIONS):
        first_hist = caches[:, offset: offset + 2 * dilation * C1].reshape(rows_here, 2 * dilation, C1)
        offset = offset + 2 * dilation * C1
        second_hist = caches[:, offset: offset + 2 * C1].reshape(rows_here, 2, C1)
        offset = offset + 2 * C1
        first_seq = jnp.concatenate([first_hist, leaky_relu(stream).astype(jnp.bfloat16)], axis=1)
        inner_out = jnp.dot(shifted_columns(first_seq, dilation, length).reshape(rows_here * length, 3 * C1), res_first[section], preferred_element_type=jnp.float32)
        second_seq = jnp.concatenate([second_hist, leaky_relu(inner_out).astype(jnp.bfloat16).reshape(rows_here, length, C1)], axis=1)
        outer_out = jnp.dot(shifted_columns(second_seq, 1, length).reshape(rows_here * length, 3 * C1), res_second[section], preferred_element_type=jnp.float32)
        stream = stream + outer_out.reshape(rows_here, length, C1)
        kept_parts.append(first_seq[:, length:].reshape(rows_here, 2 * dilation * C1))
        kept_parts.append(second_seq[:, length:].reshape(rows_here, 2 * C1))
    wave_out = stream.astype(jnp.bfloat16).reshape(rows_here, length * C1)
    fresh_cache = jnp.concatenate(kept_parts, axis=1)
    return wave_out, fresh_cache


def ranks_of(owners):
    members = owners.shape[1]
    same_owner = owners[:, :, None] == owners[:, None, :]
    earlier = jnp.arange(members)[None, :] < jnp.arange(members)[:, None]
    return jnp.sum((same_owner & earlier[None]).astype(jnp.int32), axis=2).astype(jnp.int32)


def reference(mel_rows, old_cache, new_owner, prev_owner, active, w_pre, w_up, res_first, res_second):
    new_list = new_owner[:, 0]
    prev_list = prev_owner[:, 0]
    new_rank = ranks_of(new_list.reshape(N_POOL, U_DEV)).reshape(UTT)
    prev_rank = ranks_of(prev_list.reshape(N_POOL, U_DEV)).reshape(UTT)
    home_index = (jnp.arange(UTT) // U_DEV).astype(jnp.int32)
    source_row = (prev_list * SLOTS + home_index * CAP + prev_rank).astype(jnp.int32)
    held_cache = jnp.take(old_cache, source_row, axis=0)

    def one_block(pieces):
        return vocode(pieces[0], pieces[1], w_pre, w_up, res_first, res_second)

    wave_out, fresh_cache = lax.map(one_block, (mel_rows.reshape(N_POOL, U_DEV, -1), held_cache.reshape(N_POOL, U_DEV, -1)))
    wave_out = wave_out.reshape(UTT, -1)
    fresh_cache = fresh_cache.reshape(UTT, -1)
    live_rows = (active == 1)[:, None]
    wave_features = jnp.where(live_rows, wave_out, jnp.zeros_like(wave_out))
    kept_cache = jnp.where(live_rows, fresh_cache, held_cache)
    target_row = (new_list * SLOTS + home_index * CAP + new_rank).astype(jnp.int32)
    new_cache = jnp.zeros((N_POOL * SLOTS, CACHE_W), jnp.bfloat16).at[target_row].set(kept_cache)
    return wave_features, new_cache
```

```python
import jax
import jax.numpy as jnp
from jax import lax
from jax.sharding import PartitionSpec as P

C0 = 512
C1 = 256
MELS = 80
UP = 8
FRAMES = 18
LOOK = 6


DILATIONS = (1, 3, 5)
SLOPE = 0.1


def leaky_relu(values):
    return jnp.where(values >= 0, values, SLOPE * values)


def shifted_columns(sequence, dilation, length):
    return jnp.concatenate(
        [
            sequence[:, tap_index * dilation : tap_index * dilation + length, :]
            for tap_index in range(3)
        ],
        axis=-1,
    )


def vocode(mel_block, caches, w_pre, w_up, res_first, res_second):
    rows_here = mel_block.shape[0]
    frames_in = mel_block.reshape(rows_here, FRAMES + LOOK, MELS)
    window = jnp.concatenate(
        [frames_in[:, tap_index : tap_index + FRAMES, :] for tap_index in range(LOOK + 1)], axis=-1
    )
    window = window.reshape(rows_here * FRAMES, (LOOK + 1) * MELS)
    pre_out = jnp.dot(window, w_pre, preferred_element_type=jnp.float32).reshape(
        rows_here, FRAMES, C0
    )
    pre_last = caches[:, :C0].reshape(rows_here, 1, C0)
    up_input = jnp.concatenate([pre_last, leaky_relu(pre_out).astype(jnp.bfloat16)], axis=1)
    paired = jnp.concatenate([up_input[:, :-1], up_input[:, 1:]], axis=-1).reshape(
        rows_here * FRAMES, 2 * C0
    )
    length = UP * FRAMES
    stream = jnp.dot(paired, w_up, preferred_element_type=jnp.float32).reshape(
        rows_here, length, C1
    )
    kept_parts = [up_input[:, FRAMES]]
    offset = C0
    for section, dilation in enumerate(DILATIONS):
        first_hist = caches[:, offset : offset + 2 * dilation * C1].reshape(
            rows_here, 2 * dilation, C1
        )
        offset = offset + 2 * dilation * C1
        second_hist = caches[:, offset : offset + 2 * C1].reshape(rows_here, 2, C1)
        offset = offset + 2 * C1
        first_seq = jnp.concatenate([first_hist, leaky_relu(stream).astype(jnp.bfloat16)], axis=1)
        inner_out = jnp.dot(
            shifted_columns(first_seq, dilation, length).reshape(rows_here * length, 3 * C1),
            res_first[section],
            preferred_element_type=jnp.float32,
        )
        second_seq = jnp.concatenate(
            [
                second_hist,
                leaky_relu(inner_out).astype(jnp.bfloat16).reshape(rows_here, length, C1),
            ],
            axis=1,
        )
        outer_out = jnp.dot(
            shifted_columns(second_seq, 1, length).reshape(rows_here * length, 3 * C1),
            res_second[section],
            preferred_element_type=jnp.float32,
        )
        stream = stream + outer_out.reshape(rows_here, length, C1)
        kept_parts.append(first_seq[:, length:].reshape(rows_here, 2 * dilation * C1))
        kept_parts.append(second_seq[:, length:].reshape(rows_here, 2 * C1))
    wave_out = stream.astype(jnp.bfloat16).reshape(rows_here, length * C1)
    fresh_cache = jnp.concatenate(kept_parts, axis=1)
    return (wave_out, fresh_cache)


def ranks_of(owners):
    members = owners.shape[1]
    same_owner = owners[:, :, None] == owners[:, None, :]
    earlier = jnp.arange(members)[None, :] < jnp.arange(members)[:, None]
    return jnp.sum((same_owner & earlier[None]).astype(jnp.int32), axis=2)


def on_device(
    mel_rows, old_cache, new_owner, prev_owner, active, w_pre, w_up, res_first, res_second
):
    pool_size = lax.axis_size("pool")
    position = lax.axis_index("pool")
    rows_here = mel_rows.shape[0]
    slot_total = old_cache.shape[0]
    capacity = slot_total // pool_size
    cache_width = old_cache.shape[1]
    my_new = lax.dynamic_slice_in_dim(new_owner[:, 0], position * rows_here, rows_here)
    my_prev = lax.dynamic_slice_in_dim(prev_owner[:, 0], position * rows_here, rows_here)
    my_active = lax.dynamic_slice_in_dim(active, position * rows_here, rows_here)
    my_new_rank = ranks_of(my_new[None])[0]
    my_prev_rank = ranks_of(my_prev[None])[0]
    arrived = lax.all_to_all(
        old_cache.reshape(pool_size, capacity, cache_width),
        "pool",
        split_axis=0,
        concat_axis=0,
        tiled=True,
    )
    arrived = arrived.reshape(slot_total, cache_width)
    picking = (
        (my_prev * capacity + my_prev_rank)[:, None] == jnp.arange(slot_total)[None, :]
    ).astype(jnp.bfloat16)
    held_cache = jnp.dot(picking, arrived, preferred_element_type=jnp.float32).astype(
        jnp.bfloat16
    )
    wave_out, fresh_cache = vocode(mel_rows, held_cache, w_pre, w_up, res_first, res_second)
    live_rows = (my_active == 1)[:, None]
    wave_features = jnp.where(live_rows, wave_out, jnp.zeros_like(wave_out))
    kept_cache = jnp.where(live_rows, fresh_cache, held_cache)
    slot_ids = my_new * capacity + my_new_rank
    placing = (jnp.arange(slot_total)[:, None] == slot_ids[None, :]).astype(jnp.bfloat16)
    sent_cache = jnp.dot(placing, kept_cache, preferred_element_type=jnp.float32).astype(
        jnp.bfloat16
    )
    new_cache = lax.all_to_all(
        sent_cache.reshape(pool_size, capacity, cache_width),
        "pool",
        split_axis=0,
        concat_axis=0,
        tiled=True,
    ).reshape(slot_total, cache_width)
    return (wave_features, new_cache)


def solution(mesh):
    return jax.shard_map(
        on_device,
        mesh=mesh,
        in_specs=(
            P(("grp", "pool"), None),
            P(("grp", "pool"), None),
            P("grp", None),
            P("grp", None),
            P("grp"),
            P(),
            P(),
            P(),
            P(),
        ),
        out_specs=(P(("grp", "pool"), None), P(("grp", "pool"), None)),
        check_vma=False,
    )
```

```python
import jax
import jax.numpy as jnp
from jax import lax
from jax.experimental import pallas as pl
from jax.experimental.pallas import tpu as pltpu
from jax.sharding import PartitionSpec as P

C0 = 512
C1 = 256
MELS = 80
UP = 8
FRAMES = 18
LOOK = 6


DILATIONS = (1, 3, 5)
SLOPE = 0.1
BLOCK = 16
CHUNK = 384


def leaky_relu(values):
    return jnp.where(values >= 0, values, SLOPE * values)


def vocode_kernel(
    win_ref, held_ref, act_ref, wpre_ref, wup_ref, rf_ref, rs_ref,
    wave_ref, kept_ref, x_ref, a_ref, e_ref,
):
    rows = held_ref.shape[0]
    length = UP * FRAMES
    live = act_ref[...] == 1
    win = win_ref[...].reshape(FRAMES * rows, win_ref.shape[2])
    pre = jnp.dot(win, wpre_ref[...], preferred_element_type=jnp.float32)
    pre_act = leaky_relu(pre).astype(jnp.bfloat16)
    up_input = jnp.concatenate([held_ref[:, :C0], pre_act], axis=0)
    paired = jnp.concatenate([up_input[: FRAMES * rows], up_input[rows:]], axis=1)
    prod = jnp.dot(paired, wup_ref[...], preferred_element_type=jnp.float32)
    for t in range(FRAMES):
        for j in range(UP):
            x_ref[pl.ds((UP * t + j) * rows, rows), :] = prod[
                t * rows : (t + 1) * rows, j * C1 : (j + 1) * C1
            ]
    kept_ref[:, :C0] = jnp.where(live, pre_act[(FRAMES - 1) * rows :], held_ref[:, :C0])
    offset = C0
    steps = length * rows // CHUNK
    for section, dilation in enumerate(DILATIONS):
        for p in range(2 * dilation):
            a_ref[pl.ds(p * rows, rows), :] = held_ref[:, offset + p * C1 : offset + (p + 1) * C1]
        a_off = offset
        offset = offset + 2 * dilation * C1
        for p in range(2):
            e_ref[pl.ds(p * rows, rows), :] = held_ref[:, offset + p * C1 : offset + (p + 1) * C1]
        e_off = offset
        offset = offset + 2 * C1

        def fill(c, carry, dilation=dilation):
            r = pl.multiple_of(c * CHUNK, CHUNK)
            a_ref[pl.ds(2 * dilation * rows + r, CHUNK), :] = leaky_relu(
                x_ref[pl.ds(r, CHUNK), :]
            ).astype(jnp.bfloat16)
            return carry

        lax.fori_loop(0, steps, fill, 0)

        def first(c, carry, dilation=dilation, section=section):
            r = pl.multiple_of(c * CHUNK, CHUNK)
            z = jnp.dot(
                a_ref[pl.ds(r, CHUNK), :], rf_ref[section, 0:C1, :],
                preferred_element_type=jnp.float32,
            )
            for k in (1, 2):
                z = z + jnp.dot(
                    a_ref[pl.ds(pl.multiple_of(r + k * dilation * rows, 16), CHUNK), :],
                    rf_ref[section, k * C1 : (k + 1) * C1, :],
                    preferred_element_type=jnp.float32,
                )
            e_ref[pl.ds(pl.multiple_of(2 * rows + r, 16), CHUNK), :] = leaky_relu(z).astype(
                jnp.bfloat16
            )
            return carry

        lax.fori_loop(0, steps, first, 0)

        def second(c, carry, section=section):
            r = pl.multiple_of(c * CHUNK, CHUNK)
            z = x_ref[pl.ds(r, CHUNK), :]
            for k in range(3):
                z = z + jnp.dot(
                    e_ref[pl.ds(pl.multiple_of(r + k * rows, 16), CHUNK), :],
                    rs_ref[section, k * C1 : (k + 1) * C1, :],
                    preferred_element_type=jnp.float32,
                )
            x_ref[pl.ds(r, CHUNK), :] = z
            return carry

        lax.fori_loop(0, steps, second, 0)
        for p in range(2 * dilation):
            kept_ref[:, a_off + p * C1 : a_off + (p + 1) * C1] = jnp.where(
                live,
                a_ref[pl.ds((length + p) * rows, rows), :],
                held_ref[:, a_off + p * C1 : a_off + (p + 1) * C1],
            )
        for p in range(2):
            kept_ref[:, e_off + p * C1 : e_off + (p + 1) * C1] = jnp.where(
                live,
                e_ref[pl.ds((length + p) * rows, rows), :],
                held_ref[:, e_off + p * C1 : e_off + (p + 1) * C1],
            )
    for n in range(length):
        wave_ref[:, n * C1 : (n + 1) * C1] = jnp.where(
            live, x_ref[pl.ds(n * rows, rows), :], 0.0
        ).astype(jnp.bfloat16)


def vocode(mel_block, caches, live, w_pre, w_up, res_first, res_second):
    rows_here = mel_block.shape[0]
    cache_width = caches.shape[1]
    length = UP * FRAMES
    span = (LOOK + 1) * MELS
    window = jnp.stack(
        [mel_block[:, t * MELS : t * MELS + span] for t in range(FRAMES)], axis=0
    )
    block = BLOCK
    const2 = lambda i: (0, 0)
    const3 = lambda i: (0, 0, 0)
    flops = 2 * rows_here * (FRAMES * span * C0 + FRAMES * 2 * C0 * UP * C1 + 6 * length * 3 * C1 * C1)
    wave, kept = pl.pallas_call(
        vocode_kernel,
        grid=(rows_here // block,),
        in_specs=[
            pl.BlockSpec((FRAMES, block, span), lambda i: (0, i, 0)),
            pl.BlockSpec((block, cache_width), lambda i: (i, 0)),
            pl.BlockSpec((block, 1), lambda i: (i, 0)),
            pl.BlockSpec(w_pre.shape, const2),
            pl.BlockSpec(w_up.shape, const2),
            pl.BlockSpec(res_first.shape, const3),
            pl.BlockSpec(res_second.shape, const3),
        ],
        out_specs=[
            pl.BlockSpec((block, length * C1), lambda i: (i, 0)),
            pl.BlockSpec((block, cache_width), lambda i: (i, 0)),
        ],
        out_shape=[
            jax.ShapeDtypeStruct((rows_here, length * C1), jnp.bfloat16),
            jax.ShapeDtypeStruct((rows_here, cache_width), jnp.bfloat16),
        ],
        scratch_shapes=[
            pltpu.VMEM((length * block, C1), jnp.float32),
            pltpu.VMEM(((length + 10) * block, C1), jnp.bfloat16),
            pltpu.VMEM(((length + 2) * block, C1), jnp.bfloat16),
        ],
        compiler_params=pltpu.CompilerParams(vmem_limit_bytes=60 * 1024 * 1024),
        cost_estimate=pl.CostEstimate(flops=flops, transcendentals=0, bytes_accessed=12 * 1024 * 1024),
    )(window, caches, live, w_pre, w_up, res_first, res_second)
    return wave, kept


def ranks_of(owners):
    members = owners.shape[1]
    same_owner = owners[:, :, None] == owners[:, None, :]
    earlier = jnp.arange(members)[None, :] < jnp.arange(members)[:, None]
    return jnp.sum((same_owner & earlier[None]).astype(jnp.int32), axis=2)


def on_device(
    mel_rows, old_cache, new_owner, prev_owner, active, w_pre, w_up, res_first, res_second
):
    pool_size = lax.axis_size("pool")
    position = lax.axis_index("pool")
    rows_here = mel_rows.shape[0]
    slot_total = old_cache.shape[0]
    capacity = slot_total // pool_size
    cache_width = old_cache.shape[1]
    my_new = lax.dynamic_slice_in_dim(new_owner[:, 0], position * rows_here, rows_here)
    my_prev = lax.dynamic_slice_in_dim(prev_owner[:, 0], position * rows_here, rows_here)
    my_active = lax.dynamic_slice_in_dim(active, position * rows_here, rows_here)
    my_new_rank = ranks_of(my_new[None])[0]
    my_prev_rank = ranks_of(my_prev[None])[0]
    arrived = lax.all_to_all(
        old_cache.reshape(pool_size, capacity, cache_width),
        "pool",
        split_axis=0,
        concat_axis=0,
        tiled=True,
    )
    arrived = arrived.reshape(slot_total, cache_width)
    picking = (
        (my_prev * capacity + my_prev_rank)[:, None] == jnp.arange(slot_total)[None, :]
    ).astype(jnp.bfloat16)
    held_cache = jnp.dot(picking, arrived, preferred_element_type=jnp.float32).astype(
        jnp.bfloat16
    )
    wave_features, kept_cache = vocode(
        mel_rows, held_cache, my_active[:, None], w_pre, w_up, res_first, res_second
    )
    slot_ids = my_new * capacity + my_new_rank
    placing = (jnp.arange(slot_total)[:, None] == slot_ids[None, :]).astype(jnp.bfloat16)
    sent_cache = jnp.dot(placing, kept_cache, preferred_element_type=jnp.float32).astype(
        jnp.bfloat16
    )
    new_cache = lax.all_to_all(
        sent_cache.reshape(pool_size, capacity, cache_width),
        "pool",
        split_axis=0,
        concat_axis=0,
        tiled=True,
    ).reshape(slot_total, cache_width)
    return (wave_features, new_cache)


def solution(mesh):
    return jax.shard_map(
        on_device,
        mesh=mesh,
        in_specs=(
            P(("grp", "pool"), None),
            P(("grp", "pool"), None),
            P("grp", None),
            P("grp", None),
            P("grp"),
            P(),
            P(),
            P(),
            P(),
        ),
        out_specs=(P(("grp", "pool"), None), P(("grp", "pool"), None)),
        check_vma=False,
    )
```

```python
import jax
import jax.numpy as jnp
from jax import lax
from jax.experimental import pallas as pl
from jax.experimental.pallas import tpu as pltpu
from jax.sharding import PartitionSpec as P

C0 = 512
C1 = 256
MELS = 80
UP = 8
FRAMES = 18
LOOK = 6


DILATIONS = (1, 3, 5)
SLOPE = 0.1
BLOCK = 16
CHUNK = 384


def leaky_relu(values):
    return jnp.where(values >= 0, values, SLOPE * values)


def vocode_kernel(
    win_ref, held_ref, act_ref, wpre_ref, wup_ref, rf_ref, rs_ref,
    wave_ref, kept_ref, x_ref, a_ref, e_ref,
):
    rows = held_ref.shape[0]
    length = UP * FRAMES
    live = act_ref[...] == 1
    win = win_ref[...].reshape(FRAMES * rows, win_ref.shape[2])
    pre = jnp.dot(win, wpre_ref[...], preferred_element_type=jnp.float32)
    pre_act = leaky_relu(pre).astype(jnp.bfloat16)
    up_input = jnp.concatenate([held_ref[:, :C0], pre_act], axis=0)
    paired = jnp.concatenate([up_input[: FRAMES * rows], up_input[rows:]], axis=1)
    prod = jnp.dot(paired, wup_ref[...], preferred_element_type=jnp.float32)
    for t in range(FRAMES):
        for j in range(UP):
            x_ref[pl.ds((UP * t + j) * rows, rows), :] = prod[
                t * rows : (t + 1) * rows, j * C1 : (j + 1) * C1
            ]
    kept_ref[:, :C0] = jnp.where(live, pre_act[(FRAMES - 1) * rows :], held_ref[:, :C0])
    offset = C0
    steps = length * rows // CHUNK
    for section, dilation in enumerate(DILATIONS):
        for p in range(2 * dilation):
            a_ref[pl.ds(p * rows, rows), :] = held_ref[:, offset + p * C1 : offset + (p + 1) * C1]
        a_off = offset
        offset = offset + 2 * dilation * C1
        for p in range(2):
            e_ref[pl.ds(p * rows, rows), :] = held_ref[:, offset + p * C1 : offset + (p + 1) * C1]
        e_off = offset
        offset = offset + 2 * C1

        def fill(c, carry, dilation=dilation):
            r = pl.multiple_of(c * CHUNK, CHUNK)
            a_ref[pl.ds(2 * dilation * rows + r, CHUNK), :] = leaky_relu(
                x_ref[pl.ds(r, CHUNK), :]
            ).astype(jnp.bfloat16)
            return carry

        lax.fori_loop(0, steps, fill, 0)

        def first(c, carry, dilation=dilation, section=section):
            r = pl.multiple_of(c * CHUNK, CHUNK)
            z = jnp.dot(
                a_ref[pl.ds(r, CHUNK), :], rf_ref[section, 0:C1, :],
                preferred_element_type=jnp.float32,
            )
            for k in (1, 2):
                z = z + jnp.dot(
                    a_ref[pl.ds(pl.multiple_of(r + k * dilation * rows, 16), CHUNK), :],
                    rf_ref[section, k * C1 : (k + 1) * C1, :],
                    preferred_element_type=jnp.float32,
                )
            e_ref[pl.ds(pl.multiple_of(2 * rows + r, 16), CHUNK), :] = leaky_relu(z).astype(
                jnp.bfloat16
            )
            return carry

        lax.fori_loop(0, steps, first, 0)

        def second(c, carry, section=section):
            r = pl.multiple_of(c * CHUNK, CHUNK)
            z = x_ref[pl.ds(r, CHUNK), :]
            for k in range(3):
                z = z + jnp.dot(
                    e_ref[pl.ds(pl.multiple_of(r + k * rows, 16), CHUNK), :],
                    rs_ref[section, k * C1 : (k + 1) * C1, :],
                    preferred_element_type=jnp.float32,
                )
            x_ref[pl.ds(r, CHUNK), :] = z
            return carry

        lax.fori_loop(0, steps, second, 0)
        for p in range(2 * dilation):
            kept_ref[:, a_off + p * C1 : a_off + (p + 1) * C1] = jnp.where(
                live,
                a_ref[pl.ds((length + p) * rows, rows), :],
                held_ref[:, a_off + p * C1 : a_off + (p + 1) * C1],
            )
        for p in range(2):
            kept_ref[:, e_off + p * C1 : e_off + (p + 1) * C1] = jnp.where(
                live,
                e_ref[pl.ds((length + p) * rows, rows), :],
                held_ref[:, e_off + p * C1 : e_off + (p + 1) * C1],
            )
    for n in range(length):
        wave_ref[:, n * C1 : (n + 1) * C1] = jnp.where(
            live, x_ref[pl.ds(n * rows, rows), :], 0.0
        ).astype(jnp.bfloat16)


def vocode(mel_block, caches, live, w_pre, w_up, res_first, res_second):
    rows_here = mel_block.shape[0]
    cache_width = caches.shape[1]
    length = UP * FRAMES
    span = (LOOK + 1) * MELS
    window = jnp.stack(
        [mel_block[:, t * MELS : t * MELS + span] for t in range(FRAMES)], axis=0
    )
    block = BLOCK
    const2 = lambda i: (0, 0)
    const3 = lambda i: (0, 0, 0)
    flops = 2 * rows_here * (FRAMES * span * C0 + FRAMES * 2 * C0 * UP * C1 + 6 * length * 3 * C1 * C1)
    wave, kept = pl.pallas_call(
        vocode_kernel,
        grid=(rows_here // block,),
        in_specs=[
            pl.BlockSpec((FRAMES, block, span), lambda i: (0, i, 0)),
            pl.BlockSpec((block, cache_width), lambda i: (i, 0)),
            pl.BlockSpec((block, 1), lambda i: (i, 0)),
            pl.BlockSpec(w_pre.shape, const2),
            pl.BlockSpec(w_up.shape, const2),
            pl.BlockSpec(res_first.shape, const3),
            pl.BlockSpec(res_second.shape, const3),
        ],
        out_specs=[
            pl.BlockSpec((block, length * C1), lambda i: (i, 0)),
            pl.BlockSpec((block, cache_width), lambda i: (i, 0)),
        ],
        out_shape=[
            jax.ShapeDtypeStruct((rows_here, length * C1), jnp.bfloat16),
            jax.ShapeDtypeStruct((rows_here, cache_width), jnp.bfloat16),
        ],
        scratch_shapes=[
            pltpu.VMEM((length * block, C1), jnp.float32),
            pltpu.VMEM(((length + 10) * block, C1), jnp.bfloat16),
            pltpu.VMEM(((length + 2) * block, C1), jnp.bfloat16),
        ],
        compiler_params=pltpu.CompilerParams(vmem_limit_bytes=60 * 1024 * 1024),
        cost_estimate=pl.CostEstimate(flops=flops, transcendentals=0, bytes_accessed=12 * 1024 * 1024),
    )(window, caches, live, w_pre, w_up, res_first, res_second)
    return wave, kept


def exchange_kernel(src_ref, dst_ref, send_sem, recv_sem, local_sem):
    n = send_sem.shape[0]
    cap = src_ref.shape[0] // n
    me = lax.axis_index("pool")
    barrier = pltpu.get_barrier_semaphore()
    for s in range(1, n):
        pl.semaphore_signal(barrier, 1, device_id={"pool": lax.rem(me + s, n)}, device_id_type=pl.DeviceIdType.MESH)
    pl.semaphore_wait(barrier, n - 1)
    local = pltpu.make_async_copy(
        src_ref.at[pl.ds(me * cap, cap)], dst_ref.at[pl.ds(me * cap, cap)], local_sem
    )
    local.start()
    copies = []
    for s in range(1, n):
        peer = lax.rem(me + s, n)
        copy = pltpu.make_async_remote_copy(
            src_ref=src_ref.at[pl.ds(peer * cap, cap)],
            dst_ref=dst_ref.at[pl.ds(me * cap, cap)],
            send_sem=send_sem.at[s],
            recv_sem=recv_sem.at[s],
            device_id={"pool": peer},
            device_id_type=pl.DeviceIdType.MESH,
        )
        copy.start()
        copies.append(copy)
    for copy in copies:
        copy.wait_send()
    for s in range(1, n):
        source = lax.rem(me + n - s, n)
        pltpu.make_async_remote_copy(
            src_ref=src_ref.at[pl.ds(source * cap, cap)],
            dst_ref=dst_ref.at[pl.ds(source * cap, cap)],
            send_sem=send_sem.at[s],
            recv_sem=recv_sem.at[s],
            device_id={"pool": source},
            device_id_type=pl.DeviceIdType.MESH,
        ).wait_recv()
    local.wait()


def exchange(blocks, tag):
    n = lax.axis_size("pool")
    return pl.pallas_call(
        exchange_kernel,
        in_specs=[pl.BlockSpec(memory_space=pl.ANY)],
        out_specs=pl.BlockSpec(memory_space=pl.ANY),
        out_shape=jax.ShapeDtypeStruct(blocks.shape, blocks.dtype),
        scratch_shapes=[
            pltpu.SemaphoreType.DMA((n,)),
            pltpu.SemaphoreType.DMA((n,)),
            pltpu.SemaphoreType.DMA,
        ],
        compiler_params=pltpu.CompilerParams(collective_id=tag, has_side_effects=True),
    )(blocks)


def ranks_of(owners):
    members = owners.shape[1]
    same_owner = owners[:, :, None] == owners[:, None, :]
    earlier = jnp.arange(members)[None, :] < jnp.arange(members)[:, None]
    return jnp.sum((same_owner & earlier[None]).astype(jnp.int32), axis=2)


def on_device(
    mel_rows, old_cache, new_owner, prev_owner, active, w_pre, w_up, res_first, res_second
):
    pool_size = lax.axis_size("pool")
    position = lax.axis_index("pool")
    rows_here = mel_rows.shape[0]
    slot_total = old_cache.shape[0]
    capacity = slot_total // pool_size
    cache_width = old_cache.shape[1]
    my_new = lax.dynamic_slice_in_dim(new_owner[:, 0], position * rows_here, rows_here)
    my_prev = lax.dynamic_slice_in_dim(prev_owner[:, 0], position * rows_here, rows_here)
    my_active = lax.dynamic_slice_in_dim(active, position * rows_here, rows_here)
    my_new_rank = ranks_of(my_new[None])[0]
    my_prev_rank = ranks_of(my_prev[None])[0]
    arrived = exchange(old_cache, 0)
    picking = (
        (my_prev * capacity + my_prev_rank)[:, None] == jnp.arange(slot_total)[None, :]
    ).astype(jnp.bfloat16)
    held_cache = jnp.dot(picking, arrived, preferred_element_type=jnp.float32).astype(
        jnp.bfloat16
    )
    wave_features, kept_cache = vocode(
        mel_rows, held_cache, my_active[:, None], w_pre, w_up, res_first, res_second
    )
    slot_ids = my_new * capacity + my_new_rank
    placing = (jnp.arange(slot_total)[:, None] == slot_ids[None, :]).astype(jnp.bfloat16)
    sent_cache = jnp.dot(placing, kept_cache, preferred_element_type=jnp.float32).astype(
        jnp.bfloat16
    )
    new_cache = exchange(sent_cache, 1)
    return (wave_features, new_cache)


def solution(mesh):
    return jax.shard_map(
        on_device,
        mesh=mesh,
        in_specs=(
            P(("grp", "pool"), None),
            P(("grp", "pool"), None),
            P("grp", None),
            P("grp", None),
            P("grp"),
            P(),
            P(),
            P(),
            P(),
        ),
        out_specs=(P(("grp", "pool"), None), P(("grp", "pool"), None)),
        check_vma=False,
    )
```

```python
import jax
import jax.numpy as jnp
from jax import lax
from jax.experimental import pallas as pl
from jax.experimental.pallas import tpu as pltpu
from jax.sharding import PartitionSpec as P

C0 = 512
C1 = 256
MELS = 80
UP = 8
FRAMES = 18
LOOK = 6


DILATIONS = (1, 3, 5)
SLOPE = 0.1
CHUNK = 768


def leaky_relu(values):
    return jnp.where(values >= 0, values, SLOPE * values)


MESH = pl.DeviceIdType.MESH
IN_PIECES = ((0, 1536), (1536, 3584), (3584, 6656))
OUT_PIECES = ((0, 1536), (1536, 3584), (3584, 6144), (6144, 6656))


def fused_kernel(
    mel_ref, old_ref, pick_ref, place_ref, act_ref, wpre_ref, wup_ref, rf_ref, rs_ref,
    wave_ref, new_ref,
    arrived, sendbuf, held, kept, x_ref, a_ref, e_ref,
    in_send, in_recv, in_local, out_send, out_recv, out_local,
):
    n = in_send.shape[1]
    cap = old_ref.shape[0] // n
    rows = held.shape[0]
    length = UP * FRAMES
    me = lax.axis_index("pool")

    barrier = pltpu.get_barrier_semaphore()

    def greet(s, carry):
        pl.semaphore_signal(barrier, 1, device_id={"pool": lax.rem(me + s, n)}, device_id_type=MESH)
        return carry

    lax.fori_loop(1, n, greet, 0)
    pl.semaphore_wait(barrier, n - 1)

    def start_piece(src, dst, lo, hi, sends, recvs, locals_, p):
        cols = pl.ds(lo, hi - lo)
        mine = pl.ds(pl.multiple_of(me * cap, cap), cap)
        pltpu.make_async_copy(src.at[mine, cols], dst.at[mine, cols], locals_.at[p]).start()

        def body(s, carry):
            peer = lax.rem(me + s, n)
            pltpu.make_async_remote_copy(
                src_ref=src.at[pl.ds(pl.multiple_of(peer * cap, cap), cap), cols],
                dst_ref=dst.at[mine, cols],
                send_sem=sends.at[p, s],
                recv_sem=recvs.at[p, s],
                device_id={"pool": peer},
                device_id_type=MESH,
            ).start()
            return carry

        lax.fori_loop(1, n, body, 0)

    def wait_piece(src, dst, lo, hi, sends, recvs, locals_, p):
        cols = pl.ds(lo, hi - lo)
        mine = pl.ds(pl.multiple_of(me * cap, cap), cap)

        def body(s, carry):
            peer = lax.rem(me + s, n)
            source = lax.rem(me + n - s, n)
            pltpu.make_async_remote_copy(
                src_ref=src.at[pl.ds(pl.multiple_of(peer * cap, cap), cap), cols],
                dst_ref=dst.at[mine, cols],
                send_sem=sends.at[p, s],
                recv_sem=recvs.at[p, s],
                device_id={"pool": peer},
                device_id_type=MESH,
            ).wait_send()
            pltpu.make_async_remote_copy(
                src_ref=src.at[pl.ds(pl.multiple_of(source * cap, cap), cap), cols],
                dst_ref=dst.at[pl.ds(pl.multiple_of(source * cap, cap), cap), cols],
                send_sem=sends.at[p, s],
                recv_sem=recvs.at[p, s],
                device_id={"pool": source},
                device_id_type=MESH,
            ).wait_recv()
            return carry

        lax.fori_loop(1, n, body, 0)
        pltpu.make_async_copy(src.at[mine, cols], dst.at[mine, cols], locals_.at[p]).wait()

    def fetch(p):
        wait_piece(old_ref, arrived, *IN_PIECES[p], in_send, in_recv, in_local, p)
        lo, hi = IN_PIECES[p]
        held[:, lo:hi] = jnp.dot(
            pick_ref[...], arrived[:, lo:hi], preferred_element_type=jnp.float32
        ).astype(jnp.bfloat16)

    def post(p):
        lo, hi = OUT_PIECES[p]
        sendbuf[:, lo:hi] = jnp.dot(
            place_ref[...], kept[:, lo:hi], preferred_element_type=jnp.float32
        ).astype(jnp.bfloat16)
        start_piece(sendbuf, new_ref, lo, hi, out_send, out_recv, out_local, p)

    start_piece(old_ref, arrived, *IN_PIECES[0], in_send, in_recv, in_local, 0)
    start_piece(old_ref, arrived, *IN_PIECES[1], in_send, in_recv, in_local, 1)

    live = act_ref[...] == 1
    span = MELS
    pre = jnp.dot(mel_ref[0 : FRAMES * rows, :], wpre_ref[0:span, :], preferred_element_type=jnp.float32)
    for k in range(1, LOOK + 1):
        pre = pre + jnp.dot(
            mel_ref[k * rows : (k + FRAMES) * rows, :],
            wpre_ref[k * span : (k + 1) * span, :],
            preferred_element_type=jnp.float32,
        )
    pre_act = leaky_relu(pre).astype(jnp.bfloat16)
    for j in range(UP):
        cols = slice(j * C1, (j + 1) * C1)
        part = jnp.dot(pre_act, wup_ref[C0 : 2 * C0, cols], preferred_element_type=jnp.float32)
        rest = jnp.dot(
            pre_act[: (FRAMES - 1) * rows], wup_ref[0:C0, cols], preferred_element_type=jnp.float32
        )
        x_ref[pl.ds(j * rows, rows), :] = part[0:rows]
        for t in range(1, FRAMES):
            x_ref[pl.ds((UP * t + j) * rows, rows), :] = (
                part[t * rows : (t + 1) * rows] + rest[(t - 1) * rows : t * rows]
            )

    fetch(0)
    start_piece(old_ref, arrived, *IN_PIECES[2], in_send, in_recv, in_local, 2)
    head = jnp.dot(held[:, 0:C0], wup_ref[0:C0, :], preferred_element_type=jnp.float32)
    for j in range(UP):
        x_ref[pl.ds(j * rows, rows), :] = x_ref[pl.ds(j * rows, rows), :] + head[:, j * C1 : (j + 1) * C1]
    kept[:, 0:C0] = jnp.where(live, pre_act[(FRAMES - 1) * rows :], held[:, 0:C0])

    offset = C0
    steps = length * rows // CHUNK
    for section, dilation in enumerate(DILATIONS):
        if section > 0:
            fetch(section)
        a_off = offset
        for p in range(2 * dilation):
            a_ref[pl.ds(p * rows, rows), :] = held[:, offset + p * C1 : offset + (p + 1) * C1]
        offset = offset + 2 * dilation * C1
        e_off = offset
        for p in range(2):
            e_ref[pl.ds(p * rows, rows), :] = held[:, offset + p * C1 : offset + (p + 1) * C1]
        offset = offset + 2 * C1

        def fill(c, carry, dilation=dilation):
            r = pl.multiple_of(c * CHUNK, CHUNK)
            a_ref[pl.ds(pl.multiple_of(2 * dilation * rows + r, 16), CHUNK), :] = leaky_relu(
                x_ref[pl.ds(r, CHUNK), :]
            ).astype(jnp.bfloat16)
            return carry

        lax.fori_loop(0, steps, fill, 0)
        for p in range(2 * dilation):
            kept[:, a_off + p * C1 : a_off + (p + 1) * C1] = jnp.where(
                live,
                a_ref[pl.ds((length + p) * rows, rows), :],
                held[:, a_off + p * C1 : a_off + (p + 1) * C1],
            )
        if section == 2:
            post(2)

        def first(c, carry, dilation=dilation, section=section):
            r = pl.multiple_of(c * CHUNK, CHUNK)
            z = jnp.dot(
                a_ref[pl.ds(r, CHUNK), :], rf_ref[section, 0:C1, :],
                preferred_element_type=jnp.float32,
            )
            for k in (1, 2):
                z = z + jnp.dot(
                    a_ref[pl.ds(pl.multiple_of(r + k * dilation * rows, 16), CHUNK), :],
                    rf_ref[section, k * C1 : (k + 1) * C1, :],
                    preferred_element_type=jnp.float32,
                )
            e_ref[pl.ds(pl.multiple_of(2 * rows + r, 16), CHUNK), :] = leaky_relu(z).astype(
                jnp.bfloat16
            )
            return carry

        lax.fori_loop(0, steps, first, 0)
        for p in range(2):
            kept[:, e_off + p * C1 : e_off + (p + 1) * C1] = jnp.where(
                live,
                e_ref[pl.ds((length + p) * rows, rows), :],
                held[:, e_off + p * C1 : e_off + (p + 1) * C1],
            )
        post(section if section < 2 else 3)

        def second(c, carry, section=section):
            r = pl.multiple_of(c * CHUNK, CHUNK)
            z = x_ref[pl.ds(r, CHUNK), :]
            for k in range(3):
                z = z + jnp.dot(
                    e_ref[pl.ds(pl.multiple_of(r + k * rows, 16), CHUNK), :],
                    rs_ref[section, k * C1 : (k + 1) * C1, :],
                    preferred_element_type=jnp.float32,
                )
            x_ref[pl.ds(r, CHUNK), :] = z
            return carry

        lax.fori_loop(0, steps, second, 0)
    for m in range(length):
        wave_ref[:, m * C1 : (m + 1) * C1] = jnp.where(
            live, x_ref[pl.ds(m * rows, rows), :], 0.0
        ).astype(jnp.bfloat16)
    for p in range(len(OUT_PIECES)):
        wait_piece(sendbuf, new_ref, *OUT_PIECES[p], out_send, out_recv, out_local, p)


def vocode_exchange(mel_rows, old_cache, picking, placing, live, w_pre, w_up, res_first, res_second):
    n = lax.axis_size("pool")
    rows = mel_rows.shape[0]
    slot_total, width = old_cache.shape
    length = UP * FRAMES
    mel_t = mel_rows.reshape(rows, FRAMES + LOOK, MELS).transpose(1, 0, 2).reshape(-1, MELS)
    vmem = pl.BlockSpec(memory_space=pltpu.VMEM)
    anywhere = pl.BlockSpec(memory_space=pl.ANY)
    flops = 2 * rows * (FRAMES * (LOOK + 1) * MELS * C0 + FRAMES * 2 * C0 * UP * C1 + 6 * length * 3 * C1 * C1)
    return pl.pallas_call(
        fused_kernel,
        in_specs=[vmem, anywhere] + [vmem] * 7,
        out_specs=[vmem, anywhere],
        out_shape=[
            jax.ShapeDtypeStruct((rows, length * C1), jnp.bfloat16),
            jax.ShapeDtypeStruct((slot_total, width), jnp.bfloat16),
        ],
        scratch_shapes=[
            pltpu.VMEM((slot_total, width), jnp.bfloat16),
            pltpu.VMEM((slot_total, width), jnp.bfloat16),
            pltpu.VMEM((rows, width), jnp.bfloat16),
            pltpu.VMEM((rows, width), jnp.bfloat16),
            pltpu.VMEM((length * rows, C1), jnp.float32),
            pltpu.VMEM(((length + 10) * rows, C1), jnp.bfloat16),
            pltpu.VMEM(((length + 2) * rows, C1), jnp.bfloat16),
            pltpu.SemaphoreType.DMA((len(IN_PIECES), n)),
            pltpu.SemaphoreType.DMA((len(IN_PIECES), n)),
            pltpu.SemaphoreType.DMA((len(IN_PIECES),)),
            pltpu.SemaphoreType.DMA((len(OUT_PIECES), n)),
            pltpu.SemaphoreType.DMA((len(OUT_PIECES), n)),
            pltpu.SemaphoreType.DMA((len(OUT_PIECES),)),
        ],
        compiler_params=pltpu.CompilerParams(
            collective_id=0, has_side_effects=True, vmem_limit_bytes=60 * 1024 * 1024
        ),
        cost_estimate=pl.CostEstimate(flops=flops, transcendentals=0, bytes_accessed=16 * 1024 * 1024),
    )(mel_t, old_cache, picking, placing, live, w_pre, w_up, res_first, res_second)


def ranks_of(owners):
    members = owners.shape[1]
    same_owner = owners[:, :, None] == owners[:, None, :]
    earlier = jnp.arange(members)[None, :] < jnp.arange(members)[:, None]
    return jnp.sum((same_owner & earlier[None]).astype(jnp.int32), axis=2)


def on_device(
    mel_rows, old_cache, new_owner, prev_owner, active, w_pre, w_up, res_first, res_second
):
    pool_size = lax.axis_size("pool")
    position = lax.axis_index("pool")
    rows_here = mel_rows.shape[0]
    slot_total = old_cache.shape[0]
    capacity = slot_total // pool_size
    my_new = lax.dynamic_slice_in_dim(new_owner[:, 0], position * rows_here, rows_here)
    my_prev = lax.dynamic_slice_in_dim(prev_owner[:, 0], position * rows_here, rows_here)
    my_active = lax.dynamic_slice_in_dim(active, position * rows_here, rows_here)
    my_new_rank = ranks_of(my_new[None])[0]
    my_prev_rank = ranks_of(my_prev[None])[0]
    picking = (
        (my_prev * capacity + my_prev_rank)[:, None] == jnp.arange(slot_total)[None, :]
    ).astype(jnp.bfloat16)
    slot_ids = my_new * capacity + my_new_rank
    placing = (jnp.arange(slot_total)[:, None] == slot_ids[None, :]).astype(jnp.bfloat16)
    return vocode_exchange(
        mel_rows, old_cache, picking, placing, my_active[:, None], w_pre, w_up, res_first, res_second
    )


def solution(mesh):
    return jax.shard_map(
        on_device,
        mesh=mesh,
        in_specs=(
            P(("grp", "pool"), None),
            P(("grp", "pool"), None),
            P("grp", None),
            P("grp", None),
            P("grp"),
            P(),
            P(),
            P(),
            P(),
        ),
        out_specs=(P(("grp", "pool"), None), P(("grp", "pool"), None)),
        check_vma=False,
    )
```

```python
import jax
import jax.numpy as jnp
from jax import lax
from jax.experimental import pallas as pl
from jax.experimental.pallas import tpu as pltpu
from jax.sharding import PartitionSpec as P

C0 = 512
C1 = 256
MELS = 80
UP = 8
FRAMES = 18
LOOK = 6


DILATIONS = (1, 3, 5)
SLOPE = 0.1
CHUNK = 768


def leaky_relu(values):
    return jnp.where(values >= 0, values, SLOPE * values)


MESH = pl.DeviceIdType.MESH
IN_PIECES = ((0, 1536), (1536, 3584), (3584, 6656))
OUT_PIECES = ((0, 1536), (1536, 3584), (3584, 6144), (6144, 6656))


def slot_tables(new_col, prev_col, rows, slots, cap):
    ids = lax.broadcasted_iota(jnp.int32, (rows, rows), 0)
    other = lax.broadcasted_iota(jnp.int32, (rows, rows), 1)
    diagonal = ids == other
    new_row = jnp.sum(jnp.where(diagonal, new_col, 0), axis=0, keepdims=True)
    prev_row = jnp.sum(jnp.where(diagonal, prev_col, 0), axis=0, keepdims=True)
    prev_rank = jnp.sum(
        jnp.where((prev_col == prev_row) & (other < ids), 1, 0), axis=1, keepdims=True
    )
    new_rank = jnp.sum(jnp.where((new_col == new_row) & (ids < other), 1, 0), axis=0, keepdims=True)
    picking = (
        lax.broadcasted_iota(jnp.int32, (rows, slots), 1) == prev_col * cap + prev_rank
    ).astype(jnp.bfloat16)
    placing = (
        lax.broadcasted_iota(jnp.int32, (slots, rows), 0) == new_row * cap + new_rank
    ).astype(jnp.bfloat16)
    return picking, placing


def fused_kernel(
    mel_ref, old_ref, new_owner_ref, prev_owner_ref, act_ref, wpre_ref, wup_ref, rf_ref, rs_ref,
    wave_ref, new_ref,
    arrived, sendbuf, held, kept, x_ref, a_ref, e_ref, mel_t, pick_ref, place_ref,
    in_send, in_recv, in_local, out_send, out_recv, out_local,
):
    n = in_send.shape[1]
    cap = old_ref.shape[0] // n
    rows = held.shape[0]
    length = UP * FRAMES
    me = lax.axis_index("pool")
    mine_rows = pl.ds(pl.multiple_of(me * rows, rows), rows)

    barrier = pltpu.get_barrier_semaphore()

    def greet(s, carry):
        pl.semaphore_signal(barrier, 1, device_id={"pool": lax.rem(me + s, n)}, device_id_type=MESH)
        return carry

    lax.fori_loop(1, n, greet, 0)
    pl.semaphore_wait(barrier, n - 1)

    def start_piece(src, dst, lo, hi, sends, recvs, locals_, p):
        cols = pl.ds(lo, hi - lo)
        mine = pl.ds(pl.multiple_of(me * cap, cap), cap)
        pltpu.make_async_copy(src.at[mine, cols], dst.at[mine, cols], locals_.at[p]).start()

        def body(s, carry):
            peer = lax.rem(me + s, n)
            pltpu.make_async_remote_copy(
                src_ref=src.at[pl.ds(pl.multiple_of(peer * cap, cap), cap), cols],
                dst_ref=dst.at[mine, cols],
                send_sem=sends.at[p, s],
                recv_sem=recvs.at[p, s],
                device_id={"pool": peer},
                device_id_type=MESH,
            ).start()
            return carry

        lax.fori_loop(1, n, body, 0)

    def wait_piece(src, dst, lo, hi, sends, recvs, locals_, p):
        cols = pl.ds(lo, hi - lo)
        mine = pl.ds(pl.multiple_of(me * cap, cap), cap)

        def body(s, carry):
            peer = lax.rem(me + s, n)
            source = lax.rem(me + n - s, n)
            pltpu.make_async_remote_copy(
                src_ref=src.at[pl.ds(pl.multiple_of(peer * cap, cap), cap), cols],
                dst_ref=dst.at[mine, cols],
                send_sem=sends.at[p, s],
                recv_sem=recvs.at[p, s],
                device_id={"pool": peer},
                device_id_type=MESH,
            ).wait_send()
            pltpu.make_async_remote_copy(
                src_ref=src.at[pl.ds(pl.multiple_of(source * cap, cap), cap), cols],
                dst_ref=dst.at[pl.ds(pl.multiple_of(source * cap, cap), cap), cols],
                send_sem=sends.at[p, s],
                recv_sem=recvs.at[p, s],
                device_id={"pool": source},
                device_id_type=MESH,
            ).wait_recv()
            return carry

        lax.fori_loop(1, n, body, 0)
        pltpu.make_async_copy(src.at[mine, cols], dst.at[mine, cols], locals_.at[p]).wait()

    def fetch(p):
        wait_piece(old_ref, arrived, *IN_PIECES[p], in_send, in_recv, in_local, p)
        lo, hi = IN_PIECES[p]
        held[:, lo:hi] = jnp.dot(
            pick_ref[...], arrived[:, lo:hi], preferred_element_type=jnp.float32
        ).astype(jnp.bfloat16)

    def post(p):
        lo, hi = OUT_PIECES[p]
        sendbuf[:, lo:hi] = jnp.dot(
            place_ref[...], kept[:, lo:hi], preferred_element_type=jnp.float32
        ).astype(jnp.bfloat16)
        start_piece(sendbuf, new_ref, lo, hi, out_send, out_recv, out_local, p)

    start_piece(old_ref, arrived, *IN_PIECES[0], in_send, in_recv, in_local, 0)
    start_piece(old_ref, arrived, *IN_PIECES[1], in_send, in_recv, in_local, 1)

    picking, placing = slot_tables(
        new_owner_ref[mine_rows, :], prev_owner_ref[mine_rows, :], rows, old_ref.shape[0], cap
    )
    pick_ref[...] = picking
    place_ref[...] = placing
    live = act_ref[mine_rows, :] == 1
    mel_wide = mel_ref[...].astype(jnp.float32)
    for f in range(FRAMES + LOOK):
        mel_t[f * rows : (f + 1) * rows, :] = mel_wide[:, f * MELS : (f + 1) * MELS]
    span = MELS
    pre = jnp.dot(
        mel_t[0 : FRAMES * rows, :].astype(jnp.bfloat16), wpre_ref[0:span, :],
        preferred_element_type=jnp.float32,
    )
    for k in range(1, LOOK + 1):
        pre = pre + jnp.dot(
            mel_t[k * rows : (k + FRAMES) * rows, :].astype(jnp.bfloat16),
            wpre_ref[k * span : (k + 1) * span, :],
            preferred_element_type=jnp.float32,
        )
    pre_act = leaky_relu(pre).astype(jnp.bfloat16)
    for j in range(UP):
        cols = slice(j * C1, (j + 1) * C1)
        part = jnp.dot(pre_act, wup_ref[C0 : 2 * C0, cols], preferred_element_type=jnp.float32)
        rest = jnp.dot(
            pre_act[: (FRAMES - 1) * rows], wup_ref[0:C0, cols], preferred_element_type=jnp.float32
        )
        x_ref[pl.ds(j * rows, rows), :] = part[0:rows]
        for t in range(1, FRAMES):
            x_ref[pl.ds((UP * t + j) * rows, rows), :] = (
                part[t * rows : (t + 1) * rows] + rest[(t - 1) * rows : t * rows]
            )

    fetch(0)
    start_piece(old_ref, arrived, *IN_PIECES[2], in_send, in_recv, in_local, 2)
    head = jnp.dot(held[:, 0:C0], wup_ref[0:C0, :], preferred_element_type=jnp.float32)
    for j in range(UP):
        x_ref[pl.ds(j * rows, rows), :] = x_ref[pl.ds(j * rows, rows), :] + head[:, j * C1 : (j + 1) * C1]
    kept[:, 0:C0] = jnp.where(live, pre_act[(FRAMES - 1) * rows :], held[:, 0:C0])

    offset = C0
    steps = length * rows // CHUNK
    for section, dilation in enumerate(DILATIONS):
        if section > 0:
            fetch(section)
        a_off = offset
        for p in range(2 * dilation):
            a_ref[pl.ds(p * rows, rows), :] = held[:, offset + p * C1 : offset + (p + 1) * C1]
        offset = offset + 2 * dilation * C1
        e_off = offset
        for p in range(2):
            e_ref[pl.ds(p * rows, rows), :] = held[:, offset + p * C1 : offset + (p + 1) * C1]
        offset = offset + 2 * C1

        def fill(c, carry, dilation=dilation):
            r = pl.multiple_of(c * CHUNK, CHUNK)
            a_ref[pl.ds(pl.multiple_of(2 * dilation * rows + r, 16), CHUNK), :] = leaky_relu(
                x_ref[pl.ds(r, CHUNK), :]
            ).astype(jnp.bfloat16)
            return carry

        lax.fori_loop(0, steps, fill, 0)
        for p in range(2 * dilation):
            kept[:, a_off + p * C1 : a_off + (p + 1) * C1] = jnp.where(
                live,
                a_ref[pl.ds((length + p) * rows, rows), :],
                held[:, a_off + p * C1 : a_off + (p + 1) * C1],
            )
        if section == 2:
            post(2)

        def first(c, carry, dilation=dilation, section=section):
            r = pl.multiple_of(c * CHUNK, CHUNK)
            z = jnp.dot(
                a_ref[pl.ds(r, CHUNK), :], rf_ref[section, 0:C1, :],
                preferred_element_type=jnp.float32,
            )
            for k in (1, 2):
                z = z + jnp.dot(
                    a_ref[pl.ds(pl.multiple_of(r + k * dilation * rows, 16), CHUNK), :],
                    rf_ref[section, k * C1 : (k + 1) * C1, :],
                    preferred_element_type=jnp.float32,
                )
            e_ref[pl.ds(pl.multiple_of(2 * rows + r, 16), CHUNK), :] = leaky_relu(z).astype(
                jnp.bfloat16
            )
            return carry

        lax.fori_loop(0, steps, first, 0)
        for p in range(2):
            kept[:, e_off + p * C1 : e_off + (p + 1) * C1] = jnp.where(
                live,
                e_ref[pl.ds((length + p) * rows, rows), :],
                held[:, e_off + p * C1 : e_off + (p + 1) * C1],
            )
        post(section if section < 2 else 3)

        def second(c, carry, section=section):
            r = pl.multiple_of(c * CHUNK, CHUNK)
            z = x_ref[pl.ds(r, CHUNK), :]
            for k in range(3):
                z = z + jnp.dot(
                    e_ref[pl.ds(pl.multiple_of(r + k * rows, 16), CHUNK), :],
                    rs_ref[section, k * C1 : (k + 1) * C1, :],
                    preferred_element_type=jnp.float32,
                )
            x_ref[pl.ds(r, CHUNK), :] = z
            return carry

        lax.fori_loop(0, steps, second, 0)
    for m in range(length):
        wave_ref[:, m * C1 : (m + 1) * C1] = jnp.where(
            live, x_ref[pl.ds(m * rows, rows), :], 0.0
        ).astype(jnp.bfloat16)
    for p in range(len(OUT_PIECES)):
        wait_piece(sendbuf, new_ref, *OUT_PIECES[p], out_send, out_recv, out_local, p)


def vocode_exchange(mel_rows, old_cache, new_owner, prev_owner, live, w_pre, w_up, res_first, res_second):
    n = lax.axis_size("pool")
    rows = mel_rows.shape[0]
    slot_total, width = old_cache.shape
    length = UP * FRAMES
    vmem = pl.BlockSpec(memory_space=pltpu.VMEM)
    anywhere = pl.BlockSpec(memory_space=pl.ANY)
    flops = 2 * rows * (FRAMES * (LOOK + 1) * MELS * C0 + FRAMES * 2 * C0 * UP * C1 + 6 * length * 3 * C1 * C1)
    return pl.pallas_call(
        fused_kernel,
        in_specs=[vmem, anywhere] + [vmem] * 7,
        out_specs=[vmem, anywhere],
        out_shape=[
            jax.ShapeDtypeStruct((rows, length * C1), jnp.bfloat16),
            jax.ShapeDtypeStruct((slot_total, width), jnp.bfloat16),
        ],
        scratch_shapes=[
            pltpu.VMEM((slot_total, width), jnp.bfloat16),
            pltpu.VMEM((slot_total, width), jnp.bfloat16),
            pltpu.VMEM((rows, width), jnp.bfloat16),
            pltpu.VMEM((rows, width), jnp.bfloat16),
            pltpu.VMEM((length * rows, C1), jnp.float32),
            pltpu.VMEM(((length + 10) * rows, C1), jnp.bfloat16),
            pltpu.VMEM(((length + 2) * rows, C1), jnp.bfloat16),
            pltpu.VMEM(((FRAMES + LOOK) * rows, MELS), jnp.float32),
            pltpu.VMEM((rows, slot_total), jnp.bfloat16),
            pltpu.VMEM((slot_total, rows), jnp.bfloat16),
            pltpu.SemaphoreType.DMA((len(IN_PIECES), n)),
            pltpu.SemaphoreType.DMA((len(IN_PIECES), n)),
            pltpu.SemaphoreType.DMA((len(IN_PIECES),)),
            pltpu.SemaphoreType.DMA((len(OUT_PIECES), n)),
            pltpu.SemaphoreType.DMA((len(OUT_PIECES), n)),
            pltpu.SemaphoreType.DMA((len(OUT_PIECES),)),
        ],
        compiler_params=pltpu.CompilerParams(
            collective_id=0, has_side_effects=True, vmem_limit_bytes=60 * 1024 * 1024
        ),
        cost_estimate=pl.CostEstimate(flops=flops, transcendentals=0, bytes_accessed=16 * 1024 * 1024),
    )(mel_rows, old_cache, new_owner, prev_owner, live, w_pre, w_up, res_first, res_second)


def ranks_of(owners):
    members = owners.shape[1]
    same_owner = owners[:, :, None] == owners[:, None, :]
    earlier = jnp.arange(members)[None, :] < jnp.arange(members)[:, None]
    return jnp.sum((same_owner & earlier[None]).astype(jnp.int32), axis=2)


def on_device(
    mel_rows, old_cache, new_owner, prev_owner, active, w_pre, w_up, res_first, res_second
):
    return vocode_exchange(
        mel_rows, old_cache, new_owner, prev_owner, active[:, None], w_pre, w_up, res_first, res_second
    )


def solution(mesh):
    return jax.shard_map(
        on_device,
        mesh=mesh,
        in_specs=(
            P(("grp", "pool"), None),
            P(("grp", "pool"), None),
            P("grp", None),
            P("grp", None),
            P("grp"),
            P(),
            P(),
            P(),
            P(),
        ),
        out_specs=(P(("grp", "pool"), None), P(("grp", "pool"), None)),
        check_vma=False,
    )
```

```python
import jax
import jax.numpy as jnp
from jax import lax
from jax.experimental import pallas as pl
from jax.experimental.pallas import tpu as pltpu
from jax.sharding import PartitionSpec as P

C0 = 512
C1 = 256
MELS = 80
UP = 8
FRAMES = 18
LOOK = 6


DILATIONS = (1, 3, 5)
SLOPE = 0.1
CHUNK = 768


def leaky_relu(values):
    return jnp.where(values >= 0, values, SLOPE * values)


MESH = pl.DeviceIdType.MESH
IN_PIECES = ((0, 1536), (1536, 3584), (3584, 6656))
OUT_PIECES = ((0, 1536), (1536, 3584), (3584, 6144), (6144, 6656))


def slot_tables(new_col, prev_col, rows, slots, cap):
    ids = lax.broadcasted_iota(jnp.int32, (rows, rows), 0)
    other = lax.broadcasted_iota(jnp.int32, (rows, rows), 1)
    diagonal = ids == other
    new_row = jnp.sum(jnp.where(diagonal, new_col, 0), axis=0, keepdims=True)
    prev_row = jnp.sum(jnp.where(diagonal, prev_col, 0), axis=0, keepdims=True)
    prev_rank = jnp.sum(
        jnp.where((prev_col == prev_row) & (other < ids), 1, 0), axis=1, keepdims=True
    )
    new_rank = jnp.sum(jnp.where((new_col == new_row) & (ids < other), 1, 0), axis=0, keepdims=True)
    picking = (
        lax.broadcasted_iota(jnp.int32, (rows, slots), 1) == prev_col * cap + prev_rank
    ).astype(jnp.bfloat16)
    placing = (
        lax.broadcasted_iota(jnp.int32, (slots, rows), 0) == new_row * cap + new_rank
    ).astype(jnp.bfloat16)
    return picking, placing


def fused_kernel(
    mel_ref, old_ref, table_ref, wpre_ref, wup_ref, rf_ref, rs_ref,
    wave_ref, new_ref,
    arrived, sendbuf, held, kept, x_ref, a_ref, e_ref, mel_t, pick_ref, place_ref,
    in_send, in_recv, in_local, out_send, out_recv, out_local,
):
    n = in_send.shape[1]
    cap = old_ref.shape[0] // n
    rows = held.shape[0]
    length = UP * FRAMES
    me = lax.axis_index("pool")

    barrier = pltpu.get_barrier_semaphore()

    def greet(s, carry):
        pl.semaphore_signal(barrier, 1, device_id={"pool": lax.rem(me + s, n)}, device_id_type=MESH)
        return carry

    lax.fori_loop(1, n, greet, 0)
    pl.semaphore_wait(barrier, n - 1)

    def start_piece(src, dst, lo, hi, sends, recvs, locals_, p):
        cols = pl.ds(lo, hi - lo)
        mine = pl.ds(pl.multiple_of(me * cap, cap), cap)
        pltpu.make_async_copy(src.at[mine, cols], dst.at[mine, cols], locals_.at[p]).start()

        def body(s, carry):
            peer = lax.rem(me + s, n)
            pltpu.make_async_remote_copy(
                src_ref=src.at[pl.ds(pl.multiple_of(peer * cap, cap), cap), cols],
                dst_ref=dst.at[mine, cols],
                send_sem=sends.at[p, s],
                recv_sem=recvs.at[p, s],
                device_id={"pool": peer},
                device_id_type=MESH,
            ).start()
            return carry

        lax.fori_loop(1, n, body, 0)

    def wait_piece(src, dst, lo, hi, sends, recvs, locals_, p):
        cols = pl.ds(lo, hi - lo)
        mine = pl.ds(pl.multiple_of(me * cap, cap), cap)

        def body(s, carry):
            peer = lax.rem(me + s, n)
            source = lax.rem(me + n - s, n)
            pltpu.make_async_remote_copy(
                src_ref=src.at[pl.ds(pl.multiple_of(peer * cap, cap), cap), cols],
                dst_ref=dst.at[mine, cols],
                send_sem=sends.at[p, s],
                recv_sem=recvs.at[p, s],
                device_id={"pool": peer},
                device_id_type=MESH,
            ).wait_send()
            pltpu.make_async_remote_copy(
                src_ref=src.at[pl.ds(pl.multiple_of(source * cap, cap), cap), cols],
                dst_ref=dst.at[pl.ds(pl.multiple_of(source * cap, cap), cap), cols],
                send_sem=sends.at[p, s],
                recv_sem=recvs.at[p, s],
                device_id={"pool": source},
                device_id_type=MESH,
            ).wait_recv()
            return carry

        lax.fori_loop(1, n, body, 0)
        pltpu.make_async_copy(src.at[mine, cols], dst.at[mine, cols], locals_.at[p]).wait()

    def fetch(p):
        wait_piece(old_ref, arrived, *IN_PIECES[p], in_send, in_recv, in_local, p)
        lo, hi = IN_PIECES[p]
        held[:, lo:hi] = jnp.dot(
            pick_ref[...], arrived[:, lo:hi], preferred_element_type=jnp.float32
        ).astype(jnp.bfloat16)

    def post(p):
        lo, hi = OUT_PIECES[p]
        sendbuf[:, lo:hi] = jnp.dot(
            place_ref[...], kept[:, lo:hi], preferred_element_type=jnp.float32
        ).astype(jnp.bfloat16)
        start_piece(sendbuf, new_ref, lo, hi, out_send, out_recv, out_local, p)

    start_piece(old_ref, arrived, *IN_PIECES[0], in_send, in_recv, in_local, 0)
    start_piece(old_ref, arrived, *IN_PIECES[1], in_send, in_recv, in_local, 1)

    picking, placing = slot_tables(
        table_ref[:, 0:1], table_ref[:, 1:2], rows, old_ref.shape[0], cap
    )
    pick_ref[...] = picking
    place_ref[...] = placing
    live = table_ref[:, 2:3] == 1
    mel_wide = mel_ref[...].astype(jnp.float32)
    for f in range(FRAMES + LOOK):
        mel_t[f * rows : (f + 1) * rows, :] = mel_wide[:, f * MELS : (f + 1) * MELS]
    span = MELS
    pre = jnp.dot(
        mel_t[0 : FRAMES * rows, :].astype(jnp.bfloat16), wpre_ref[0:span, :],
        preferred_element_type=jnp.float32,
    )
    for k in range(1, LOOK + 1):
        pre = pre + jnp.dot(
            mel_t[k * rows : (k + FRAMES) * rows, :].astype(jnp.bfloat16),
            wpre_ref[k * span : (k + 1) * span, :],
            preferred_element_type=jnp.float32,
        )
    pre_act = leaky_relu(pre).astype(jnp.bfloat16)
    for j in range(UP):
        cols = slice(j * C1, (j + 1) * C1)
        part = jnp.dot(pre_act, wup_ref[C0 : 2 * C0, cols], preferred_element_type=jnp.float32)
        rest = jnp.dot(
            pre_act[: (FRAMES - 1) * rows], wup_ref[0:C0, cols], preferred_element_type=jnp.float32
        )
        x_ref[pl.ds(j * rows, rows), :] = part[0:rows]
        for t in range(1, FRAMES):
            x_ref[pl.ds((UP * t + j) * rows, rows), :] = (
                part[t * rows : (t + 1) * rows] + rest[(t - 1) * rows : t * rows]
            )

    fetch(0)
    start_piece(old_ref, arrived, *IN_PIECES[2], in_send, in_recv, in_local, 2)
    head = jnp.dot(held[:, 0:C0], wup_ref[0:C0, :], preferred_element_type=jnp.float32)
    for j in range(UP):
        x_ref[pl.ds(j * rows, rows), :] = x_ref[pl.ds(j * rows, rows), :] + head[:, j * C1 : (j + 1) * C1]
    kept[:, 0:C0] = jnp.where(live, pre_act[(FRAMES - 1) * rows :], held[:, 0:C0])

    offset = C0
    steps = length * rows // CHUNK
    for section, dilation in enumerate(DILATIONS):
        if section > 0:
            fetch(section)
        a_off = offset
        for p in range(2 * dilation):
            a_ref[pl.ds(p * rows, rows), :] = held[:, offset + p * C1 : offset + (p + 1) * C1]
        offset = offset + 2 * dilation * C1
        e_off = offset
        for p in range(2):
            e_ref[pl.ds(p * rows, rows), :] = held[:, offset + p * C1 : offset + (p + 1) * C1]
        offset = offset + 2 * C1

        def fill(c, carry, dilation=dilation):
            r = pl.multiple_of(c * CHUNK, CHUNK)
            a_ref[pl.ds(pl.multiple_of(2 * dilation * rows + r, 16), CHUNK), :] = leaky_relu(
                x_ref[pl.ds(r, CHUNK), :]
            ).astype(jnp.bfloat16)
            return carry

        lax.fori_loop(0, steps, fill, 0)
        for p in range(2 * dilation):
            kept[:, a_off + p * C1 : a_off + (p + 1) * C1] = jnp.where(
                live,
                a_ref[pl.ds((length + p) * rows, rows), :],
                held[:, a_off + p * C1 : a_off + (p + 1) * C1],
            )
        if section == 2:
            post(2)

        def first(c, carry, dilation=dilation, section=section):
            r = pl.multiple_of(c * CHUNK, CHUNK)
            z = jnp.dot(
                a_ref[pl.ds(r, CHUNK), :], rf_ref[section, 0:C1, :],
                preferred_element_type=jnp.float32,
            )
            for k in (1, 2):
                z = z + jnp.dot(
                    a_ref[pl.ds(pl.multiple_of(r + k * dilation * rows, 16), CHUNK), :],
                    rf_ref[section, k * C1 : (k + 1) * C1, :],
                    preferred_element_type=jnp.float32,
                )
            e_ref[pl.ds(pl.multiple_of(2 * rows + r, 16), CHUNK), :] = leaky_relu(z).astype(
                jnp.bfloat16
            )
            return carry

        lax.fori_loop(0, steps, first, 0)
        for p in range(2):
            kept[:, e_off + p * C1 : e_off + (p + 1) * C1] = jnp.where(
                live,
                e_ref[pl.ds((length + p) * rows, rows), :],
                held[:, e_off + p * C1 : e_off + (p + 1) * C1],
            )
        post(section if section < 2 else 3)

        def second(c, carry, section=section):
            r = pl.multiple_of(c * CHUNK, CHUNK)
            z = x_ref[pl.ds(r, CHUNK), :]
            for k in range(3):
                z = z + jnp.dot(
                    e_ref[pl.ds(pl.multiple_of(r + k * rows, 16), CHUNK), :],
                    rs_ref[section, k * C1 : (k + 1) * C1, :],
                    preferred_element_type=jnp.float32,
                )
            x_ref[pl.ds(r, CHUNK), :] = z
            return carry

        lax.fori_loop(0, steps, second, 0)
    for m in range(length):
        wave_ref[:, m * C1 : (m + 1) * C1] = jnp.where(
            live, x_ref[pl.ds(m * rows, rows), :], 0.0
        ).astype(jnp.bfloat16)
    for p in range(len(OUT_PIECES)):
        wait_piece(sendbuf, new_ref, *OUT_PIECES[p], out_send, out_recv, out_local, p)


def vocode_exchange(mel_rows, old_cache, table, w_pre, w_up, res_first, res_second):
    n = lax.axis_size("pool")
    rows = mel_rows.shape[0]
    slot_total, width = old_cache.shape
    length = UP * FRAMES
    vmem = pl.BlockSpec(memory_space=pltpu.VMEM)
    anywhere = pl.BlockSpec(memory_space=pl.ANY)
    flops = 2 * rows * (FRAMES * (LOOK + 1) * MELS * C0 + FRAMES * 2 * C0 * UP * C1 + 6 * length * 3 * C1 * C1)
    return pl.pallas_call(
        fused_kernel,
        in_specs=[vmem, anywhere] + [vmem] * 5,
        out_specs=[vmem, anywhere],
        out_shape=[
            jax.ShapeDtypeStruct((rows, length * C1), jnp.bfloat16),
            jax.ShapeDtypeStruct((slot_total, width), jnp.bfloat16),
        ],
        scratch_shapes=[
            pltpu.VMEM((slot_total, width), jnp.bfloat16),
            pltpu.VMEM((slot_total, width), jnp.bfloat16),
            pltpu.VMEM((rows, width), jnp.bfloat16),
            pltpu.VMEM((rows, width), jnp.bfloat16),
            pltpu.VMEM((length * rows, C1), jnp.float32),
            pltpu.VMEM(((length + 10) * rows, C1), jnp.bfloat16),
            pltpu.VMEM(((length + 2) * rows, C1), jnp.bfloat16),
            pltpu.VMEM(((FRAMES + LOOK) * rows, MELS), jnp.float32),
            pltpu.VMEM((rows, slot_total), jnp.bfloat16),
            pltpu.VMEM((slot_total, rows), jnp.bfloat16),
            pltpu.SemaphoreType.DMA((len(IN_PIECES), n)),
            pltpu.SemaphoreType.DMA((len(IN_PIECES), n)),
            pltpu.SemaphoreType.DMA((len(IN_PIECES),)),
            pltpu.SemaphoreType.DMA((len(OUT_PIECES), n)),
            pltpu.SemaphoreType.DMA((len(OUT_PIECES), n)),
            pltpu.SemaphoreType.DMA((len(OUT_PIECES),)),
        ],
        compiler_params=pltpu.CompilerParams(
            collective_id=0, has_side_effects=True, vmem_limit_bytes=60 * 1024 * 1024
        ),
        cost_estimate=pl.CostEstimate(flops=flops, transcendentals=0, bytes_accessed=16 * 1024 * 1024),
    )(mel_rows, old_cache, table, w_pre, w_up, res_first, res_second)


def ranks_of(owners):
    members = owners.shape[1]
    same_owner = owners[:, :, None] == owners[:, None, :]
    earlier = jnp.arange(members)[None, :] < jnp.arange(members)[:, None]
    return jnp.sum((same_owner & earlier[None]).astype(jnp.int32), axis=2)


def on_device(
    mel_rows, old_cache, new_owner, prev_owner, active, w_pre, w_up, res_first, res_second
):
    rows = mel_rows.shape[0]
    start = lax.axis_index("pool") * rows
    table = jnp.concatenate(
        [
            lax.dynamic_slice_in_dim(new_owner, start, rows),
            lax.dynamic_slice_in_dim(prev_owner, start, rows),
            lax.dynamic_slice_in_dim(active, start, rows)[:, None],
        ],
        axis=1,
    )
    return vocode_exchange(mel_rows, old_cache, table, w_pre, w_up, res_first, res_second)


def solution(mesh):
    return jax.shard_map(
        on_device,
        mesh=mesh,
        in_specs=(
            P(("grp", "pool"), None),
            P(("grp", "pool"), None),
            P("grp", None),
            P("grp", None),
            P("grp"),
            P(),
            P(),
            P(),
            P(),
        ),
        out_specs=(P(("grp", "pool"), None), P(("grp", "pool"), None)),
        check_vma=False,
    )
```

```python
import jax
import jax.numpy as jnp
from jax import lax
from jax.experimental import pallas as pl
from jax.experimental.pallas import tpu as pltpu
from jax.sharding import PartitionSpec as P

C0 = 512
C1 = 256
MELS = 80
UP = 8
FRAMES = 18
LOOK = 6


DILATIONS = (1, 3, 5)
SLOPE = 0.1
CHUNK = 768


def leaky_relu(values):
    return jnp.where(values >= 0, values, SLOPE * values)


MESH = pl.DeviceIdType.MESH
IN_PIECES = ((0, 1536), (1536, 3584), (3584, 6656))
OUT_PIECES = ((0, 1536), (1536, 3584), (3584, 6144), (6144, 6656))


def slot_tables(new_col, prev_col, rows, slots, cap):
    ids = lax.broadcasted_iota(jnp.int32, (rows, rows), 0)
    other = lax.broadcasted_iota(jnp.int32, (rows, rows), 1)
    diagonal = ids == other
    new_row = jnp.sum(jnp.where(diagonal, new_col, 0), axis=0, keepdims=True)
    prev_row = jnp.sum(jnp.where(diagonal, prev_col, 0), axis=0, keepdims=True)
    prev_rank = jnp.sum(
        jnp.where((prev_col == prev_row) & (other < ids), 1, 0), axis=1, keepdims=True
    )
    new_rank = jnp.sum(jnp.where((new_col == new_row) & (ids < other), 1, 0), axis=0, keepdims=True)
    picking = (
        lax.broadcasted_iota(jnp.int32, (rows, slots), 1) == prev_col * cap + prev_rank
    ).astype(jnp.bfloat16)
    placing = (
        lax.broadcasted_iota(jnp.int32, (slots, rows), 0) == new_row * cap + new_rank
    ).astype(jnp.bfloat16)
    return picking, placing


def fused_kernel(
    mel_ref, old_ref, table_ref, wpre_ref, wup_ref, rf_ref, rs_ref,
    wave_ref, new_ref,
    arrived, sendbuf, held, kept, x_ref, a_ref, e_ref, mel_t, pick_ref, place_ref,
    in_send, in_recv, in_local, out_send, out_recv, out_local,
):
    n = in_send.shape[1]
    cap = old_ref.shape[0] // n
    rows = held.shape[0]
    length = UP * FRAMES
    me = lax.axis_index("pool")

    barrier = pltpu.get_barrier_semaphore()

    def greet(s, carry):
        pl.semaphore_signal(barrier, 1, device_id={"pool": lax.rem(me + s, n)}, device_id_type=MESH)
        return carry

    lax.fori_loop(1, n, greet, 0)
    pl.semaphore_wait(barrier, n - 1)

    def start_piece(src, dst, lo, hi, sends, recvs, locals_, p):
        cols = pl.ds(lo, hi - lo)
        mine = pl.ds(pl.multiple_of(me * cap, cap), cap)
        pltpu.make_async_copy(src.at[mine, cols], dst.at[mine, cols], locals_.at[p]).start()

        def body(s, carry):
            peer = lax.rem(me + s, n)
            pltpu.make_async_remote_copy(
                src_ref=src.at[pl.ds(pl.multiple_of(peer * cap, cap), cap), cols],
                dst_ref=dst.at[mine, cols],
                send_sem=sends.at[p, s],
                recv_sem=recvs.at[p, s],
                device_id={"pool": peer},
                device_id_type=MESH,
            ).start()
            return carry

        lax.fori_loop(1, n, body, 0)

    def wait_piece(src, dst, lo, hi, sends, recvs, locals_, p):
        cols = pl.ds(lo, hi - lo)
        mine = pl.ds(pl.multiple_of(me * cap, cap), cap)

        def body(s, carry):
            peer = lax.rem(me + s, n)
            source = lax.rem(me + n - s, n)
            pltpu.make_async_remote_copy(
                src_ref=src.at[pl.ds(pl.multiple_of(peer * cap, cap), cap), cols],
                dst_ref=dst.at[mine, cols],
                send_sem=sends.at[p, s],
                recv_sem=recvs.at[p, s],
                device_id={"pool": peer},
                device_id_type=MESH,
            ).wait_send()
            pltpu.make_async_remote_copy(
                src_ref=src.at[pl.ds(pl.multiple_of(source * cap, cap), cap), cols],
                dst_ref=dst.at[pl.ds(pl.multiple_of(source * cap, cap), cap), cols],
                send_sem=sends.at[p, s],
                recv_sem=recvs.at[p, s],
                device_id={"pool": source},
                device_id_type=MESH,
            ).wait_recv()
            return carry

        lax.fori_loop(1, n, body, 0)
        pltpu.make_async_copy(src.at[mine, cols], dst.at[mine, cols], locals_.at[p]).wait()

    def fetch(p):
        wait_piece(old_ref, arrived, *IN_PIECES[p], in_send, in_recv, in_local, p)
        lo, hi = IN_PIECES[p]
        held[:, lo:hi] = jnp.dot(
            pick_ref[...], arrived[:, lo:hi], preferred_element_type=jnp.float32
        ).astype(jnp.bfloat16)

    def post(p):
        lo, hi = OUT_PIECES[p]
        sendbuf[:, lo:hi] = jnp.dot(
            place_ref[...], kept[:, lo:hi], preferred_element_type=jnp.float32
        ).astype(jnp.bfloat16)
        start_piece(sendbuf, new_ref, lo, hi, out_send, out_recv, out_local, p)

    start_piece(old_ref, arrived, *IN_PIECES[0], in_send, in_recv, in_local, 0)
    start_piece(old_ref, arrived, *IN_PIECES[1], in_send, in_recv, in_local, 1)

    picking, placing = slot_tables(
        table_ref[:, 0:1], table_ref[:, 1:2], rows, old_ref.shape[0], cap
    )
    pick_ref[...] = picking
    place_ref[...] = placing
    live = table_ref[:, 2:3] == 1
    mel_wide = mel_ref[...].astype(jnp.float32)
    for f in range(FRAMES + LOOK):
        mel_t[f * rows : (f + 1) * rows, :] = mel_wide[:, f * MELS : (f + 1) * MELS]
    span = MELS
    pre = jnp.dot(
        mel_t[0 : FRAMES * rows, :].astype(jnp.bfloat16), wpre_ref[0:span, :],
        preferred_element_type=jnp.float32,
    )
    for k in range(1, LOOK + 1):
        pre = pre + jnp.dot(
            mel_t[k * rows : (k + FRAMES) * rows, :].astype(jnp.bfloat16),
            wpre_ref[k * span : (k + 1) * span, :],
            preferred_element_type=jnp.float32,
        )
    pre_act = leaky_relu(pre).astype(jnp.bfloat16)
    for j in range(UP):
        cols = slice(j * C1, (j + 1) * C1)
        part = jnp.dot(pre_act, wup_ref[C0 : 2 * C0, cols], preferred_element_type=jnp.float32)
        rest = jnp.dot(
            pre_act[: (FRAMES - 1) * rows], wup_ref[0:C0, cols], preferred_element_type=jnp.float32
        )
        x_ref[pl.ds(j * rows, rows), :] = part[0:rows]
        for t in range(1, FRAMES):
            slab = part[t * rows : (t + 1) * rows] + rest[(t - 1) * rows : t * rows]
            x_ref[pl.ds((UP * t + j) * rows, rows), :] = slab
            a_ref[pl.ds((2 * DILATIONS[0] + UP * t + j) * rows, rows), :] = leaky_relu(slab).astype(
                jnp.bfloat16
            )

    fetch(0)
    start_piece(old_ref, arrived, *IN_PIECES[2], in_send, in_recv, in_local, 2)
    head = jnp.dot(held[:, 0:C0], wup_ref[0:C0, :], preferred_element_type=jnp.float32)
    for j in range(UP):
        slab = x_ref[pl.ds(j * rows, rows), :] + head[:, j * C1 : (j + 1) * C1]
        x_ref[pl.ds(j * rows, rows), :] = slab
        a_ref[pl.ds((2 * DILATIONS[0] + j) * rows, rows), :] = leaky_relu(slab).astype(jnp.bfloat16)
    kept[:, 0:C0] = jnp.where(live, pre_act[(FRAMES - 1) * rows :], held[:, 0:C0])

    offset = C0
    steps = length * rows // CHUNK
    for section, dilation in enumerate(DILATIONS):
        if section > 0:
            fetch(section)
        a_off = offset
        for p in range(2 * dilation):
            a_ref[pl.ds(p * rows, rows), :] = held[:, offset + p * C1 : offset + (p + 1) * C1]
        offset = offset + 2 * dilation * C1
        e_off = offset
        for p in range(2):
            e_ref[pl.ds(p * rows, rows), :] = held[:, offset + p * C1 : offset + (p + 1) * C1]
        offset = offset + 2 * C1

        def fill(c, carry, dilation=dilation):
            r = pl.multiple_of(c * CHUNK, CHUNK)
            a_ref[pl.ds(pl.multiple_of(2 * dilation * rows + r, 16), CHUNK), :] = leaky_relu(
                x_ref[pl.ds(r, CHUNK), :]
            ).astype(jnp.bfloat16)
            return carry

        for p in range(2 * dilation):
            kept[:, a_off + p * C1 : a_off + (p + 1) * C1] = jnp.where(
                live,
                a_ref[pl.ds((length + p) * rows, rows), :],
                held[:, a_off + p * C1 : a_off + (p + 1) * C1],
            )
        if section == 2:
            post(2)

        def first(c, carry, dilation=dilation, section=section):
            r = pl.multiple_of(c * CHUNK, CHUNK)
            z = jnp.dot(
                a_ref[pl.ds(r, CHUNK), :], rf_ref[section, 0:C1, :],
                preferred_element_type=jnp.float32,
            )
            for k in (1, 2):
                z = z + jnp.dot(
                    a_ref[pl.ds(pl.multiple_of(r + k * dilation * rows, 16), CHUNK), :],
                    rf_ref[section, k * C1 : (k + 1) * C1, :],
                    preferred_element_type=jnp.float32,
                )
            e_ref[pl.ds(pl.multiple_of(2 * rows + r, 16), CHUNK), :] = leaky_relu(z).astype(
                jnp.bfloat16
            )
            return carry

        lax.fori_loop(0, steps, first, 0)
        for p in range(2):
            kept[:, e_off + p * C1 : e_off + (p + 1) * C1] = jnp.where(
                live,
                e_ref[pl.ds((length + p) * rows, rows), :],
                held[:, e_off + p * C1 : e_off + (p + 1) * C1],
            )
        post(section if section < 2 else 3)

        def second(c, carry, section=section):
            r = pl.multiple_of(c * CHUNK, CHUNK)
            z = x_ref[pl.ds(r, CHUNK), :]
            for k in range(3):
                z = z + jnp.dot(
                    e_ref[pl.ds(pl.multiple_of(r + k * rows, 16), CHUNK), :],
                    rs_ref[section, k * C1 : (k + 1) * C1, :],
                    preferred_element_type=jnp.float32,
                )
            x_ref[pl.ds(r, CHUNK), :] = z
            if section + 1 < len(DILATIONS):
                ahead = 2 * DILATIONS[section + 1] * rows
                a_ref[pl.ds(pl.multiple_of(ahead + r, 16), CHUNK), :] = leaky_relu(z).astype(
                    jnp.bfloat16
                )
            return carry

        if section + 1 < len(DILATIONS):
            lax.fori_loop(0, steps, second, 0)
        else:
            for c in range(steps):
                second(c, 0)
                z = x_ref[c * CHUNK : (c + 1) * CHUNK, :]
                for m in range(CHUNK // rows):
                    sample = c * CHUNK // rows + m
                    wave_ref[:, sample * C1 : (sample + 1) * C1] = jnp.where(
                        live, z[m * rows : (m + 1) * rows], 0.0
                    ).astype(jnp.bfloat16)
    for p in range(len(OUT_PIECES)):
        wait_piece(sendbuf, new_ref, *OUT_PIECES[p], out_send, out_recv, out_local, p)


def vocode_exchange(mel_rows, old_cache, table, w_pre, w_up, res_first, res_second):
    n = lax.axis_size("pool")
    rows = mel_rows.shape[0]
    slot_total, width = old_cache.shape
    length = UP * FRAMES
    vmem = pl.BlockSpec(memory_space=pltpu.VMEM)
    anywhere = pl.BlockSpec(memory_space=pl.ANY)
    flops = 2 * rows * (FRAMES * (LOOK + 1) * MELS * C0 + FRAMES * 2 * C0 * UP * C1 + 6 * length * 3 * C1 * C1)
    return pl.pallas_call(
        fused_kernel,
        in_specs=[vmem, anywhere] + [vmem] * 5,
        out_specs=[vmem, anywhere],
        out_shape=[
            jax.ShapeDtypeStruct((rows, length * C1), jnp.bfloat16),
            jax.ShapeDtypeStruct((slot_total, width), jnp.bfloat16),
        ],
        scratch_shapes=[
            pltpu.VMEM((slot_total, width), jnp.bfloat16),
            pltpu.VMEM((slot_total, width), jnp.bfloat16),
            pltpu.VMEM((rows, width), jnp.bfloat16),
            pltpu.VMEM((rows, width), jnp.bfloat16),
            pltpu.VMEM((length * rows, C1), jnp.float32),
            pltpu.VMEM(((length + 10) * rows, C1), jnp.bfloat16),
            pltpu.VMEM(((length + 2) * rows, C1), jnp.bfloat16),
            pltpu.VMEM(((FRAMES + LOOK) * rows, MELS), jnp.float32),
            pltpu.VMEM((rows, slot_total), jnp.bfloat16),
            pltpu.VMEM((slot_total, rows), jnp.bfloat16),
            pltpu.SemaphoreType.DMA((len(IN_PIECES), n)),
            pltpu.SemaphoreType.DMA((len(IN_PIECES), n)),
            pltpu.SemaphoreType.DMA((len(IN_PIECES),)),
            pltpu.SemaphoreType.DMA((len(OUT_PIECES), n)),
            pltpu.SemaphoreType.DMA((len(OUT_PIECES), n)),
            pltpu.SemaphoreType.DMA((len(OUT_PIECES),)),
        ],
        compiler_params=pltpu.CompilerParams(
            collective_id=0, has_side_effects=True, vmem_limit_bytes=60 * 1024 * 1024
        ),
        cost_estimate=pl.CostEstimate(flops=flops, transcendentals=0, bytes_accessed=16 * 1024 * 1024),
    )(mel_rows, old_cache, table, w_pre, w_up, res_first, res_second)


def ranks_of(owners):
    members = owners.shape[1]
    same_owner = owners[:, :, None] == owners[:, None, :]
    earlier = jnp.arange(members)[None, :] < jnp.arange(members)[:, None]
    return jnp.sum((same_owner & earlier[None]).astype(jnp.int32), axis=2)


def on_device(
    mel_rows, old_cache, new_owner, prev_owner, active, w_pre, w_up, res_first, res_second
):
    rows = mel_rows.shape[0]
    start = lax.axis_index("pool") * rows
    table = jnp.concatenate(
        [
            lax.dynamic_slice_in_dim(new_owner, start, rows),
            lax.dynamic_slice_in_dim(prev_owner, start, rows),
            lax.dynamic_slice_in_dim(active, start, rows)[:, None],
        ],
        axis=1,
    )
    return vocode_exchange(mel_rows, old_cache, table, w_pre, w_up, res_first, res_second)


def solution(mesh):
    return jax.shard_map(
        on_device,
        mesh=mesh,
        in_specs=(
            P(("grp", "pool"), None),
            P(("grp", "pool"), None),
            P("grp", None),
            P("grp", None),
            P("grp"),
            P(),
            P(),
            P(),
            P(),
        ),
        out_specs=(P(("grp", "pool"), None), P(("grp", "pool"), None)),
        check_vma=False,
    )
```

```python
import jax
import jax.numpy as jnp
from jax import lax
from jax.experimental import pallas as pl
from jax.experimental.pallas import tpu as pltpu
from jax.sharding import PartitionSpec as P

C0 = 512
C1 = 256
MELS = 80
UP = 8
FRAMES = 18
LOOK = 6


DILATIONS = (1, 3, 5)
SLOPE = 0.1
CHUNK = 768


def leaky_relu(values):
    return jnp.where(values >= 0, values, SLOPE * values)


MESH = pl.DeviceIdType.MESH
IN_PIECES = ((0, 1536), (1536, 3584), (3584, 6656))
OUT_PIECES = ((0, 1536), (1536, 3584), (3584, 6144), (6144, 6656))


def slot_tables(new_ref, prev_ref, act_ref, base, rows, slots, cap):
    column = lax.broadcasted_iota(jnp.int32, (rows, 1), 0)
    row = lax.broadcasted_iota(jnp.int32, (1, rows), 1)
    new_col = jnp.zeros((rows, 1), jnp.int32)
    new_row = jnp.zeros((1, rows), jnp.int32)
    prev_col = jnp.zeros((rows, 1), jnp.int32)
    prev_row = jnp.zeros((1, rows), jnp.int32)
    act_col = jnp.zeros((rows, 1), jnp.int32)
    for u in range(rows):
        new_u = new_ref[base + u]
        prev_u = prev_ref[base + u]
        new_col = jnp.where(column == u, new_u, new_col)
        new_row = jnp.where(row == u, new_u, new_row)
        prev_col = jnp.where(column == u, prev_u, prev_col)
        prev_row = jnp.where(row == u, prev_u, prev_row)
        act_col = jnp.where(column == u, act_ref[base + u], act_col)
    ids = lax.broadcasted_iota(jnp.int32, (rows, rows), 0)
    other = lax.broadcasted_iota(jnp.int32, (rows, rows), 1)
    prev_rank = jnp.sum(
        jnp.where((prev_col == prev_row) & (other < ids), 1, 0), axis=1, keepdims=True
    )
    new_rank = jnp.sum(jnp.where((new_col == new_row) & (ids < other), 1, 0), axis=0, keepdims=True)
    picking = (
        lax.broadcasted_iota(jnp.int32, (rows, slots), 1) == prev_col * cap + prev_rank
    ).astype(jnp.bfloat16)
    placing = (
        lax.broadcasted_iota(jnp.int32, (slots, rows), 0) == new_row * cap + new_rank
    ).astype(jnp.bfloat16)
    return picking, placing, act_col == 1


def fused_kernel(
    mel_ref, old_ref, new_owner_ref, prev_owner_ref, active_ref, wpre_ref, wup_ref, rf_ref, rs_ref,
    wave_ref, new_ref,
    arrived, sendbuf, held, kept, x_ref, a_ref, e_ref, mel_t, pick_ref, place_ref,
    in_send, in_recv, in_local, out_send, out_recv, out_local,
):
    n = in_send.shape[1]
    cap = old_ref.shape[0] // n
    rows = held.shape[0]
    length = UP * FRAMES
    me = lax.axis_index("pool")

    barrier = pltpu.get_barrier_semaphore()

    def greet(s, carry):
        pl.semaphore_signal(barrier, 1, device_id={"pool": lax.rem(me + s, n)}, device_id_type=MESH)
        return carry

    lax.fori_loop(1, n, greet, 0)
    pl.semaphore_wait(barrier, n - 1)

    def start_piece(src, dst, lo, hi, sends, recvs, locals_, p):
        cols = pl.ds(lo, hi - lo)
        mine = pl.ds(pl.multiple_of(me * cap, cap), cap)
        pltpu.make_async_copy(src.at[mine, cols], dst.at[mine, cols], locals_.at[p]).start()

        def body(i, carry):
            s = n - i
            peer = lax.rem(me + s, n)
            pltpu.make_async_remote_copy(
                src_ref=src.at[pl.ds(pl.multiple_of(peer * cap, cap), cap), cols],
                dst_ref=dst.at[mine, cols],
                send_sem=sends.at[p, s],
                recv_sem=recvs.at[p, s],
                device_id={"pool": peer},
                device_id_type=MESH,
            ).start()
            return carry

        lax.fori_loop(1, n, body, 0)

    def wait_piece(src, dst, lo, hi, sends, recvs, locals_, p):
        cols = pl.ds(lo, hi - lo)
        mine = pl.ds(pl.multiple_of(me * cap, cap), cap)

        def body(s, carry):
            peer = lax.rem(me + s, n)
            source = lax.rem(me + n - s, n)
            pltpu.make_async_remote_copy(
                src_ref=src.at[pl.ds(pl.multiple_of(peer * cap, cap), cap), cols],
                dst_ref=dst.at[mine, cols],
                send_sem=sends.at[p, s],
                recv_sem=recvs.at[p, s],
                device_id={"pool": peer},
                device_id_type=MESH,
            ).wait_send()
            pltpu.make_async_remote_copy(
                src_ref=src.at[pl.ds(pl.multiple_of(source * cap, cap), cap), cols],
                dst_ref=dst.at[pl.ds(pl.multiple_of(source * cap, cap), cap), cols],
                send_sem=sends.at[p, s],
                recv_sem=recvs.at[p, s],
                device_id={"pool": source},
                device_id_type=MESH,
            ).wait_recv()
            return carry

        lax.fori_loop(1, n, body, 0)
        pltpu.make_async_copy(src.at[mine, cols], dst.at[mine, cols], locals_.at[p]).wait()

    def fetch(p):
        wait_piece(old_ref, arrived, *IN_PIECES[p], in_send, in_recv, in_local, p)
        lo, hi = IN_PIECES[p]
        held[:, lo:hi] = jnp.dot(
            pick_ref[...], arrived[:, lo:hi], preferred_element_type=jnp.float32
        ).astype(jnp.bfloat16)

    def post(p):
        lo, hi = OUT_PIECES[p]
        sendbuf[:, lo:hi] = jnp.dot(
            place_ref[...], kept[:, lo:hi], preferred_element_type=jnp.float32
        ).astype(jnp.bfloat16)
        start_piece(sendbuf, new_ref, lo, hi, out_send, out_recv, out_local, p)

    start_piece(old_ref, arrived, *IN_PIECES[0], in_send, in_recv, in_local, 0)
    start_piece(old_ref, arrived, *IN_PIECES[1], in_send, in_recv, in_local, 1)

    picking, placing, live = slot_tables(
        new_owner_ref, prev_owner_ref, active_ref, me * rows, rows, old_ref.shape[0], cap
    )
    pick_ref[...] = picking
    place_ref[...] = placing
    mel_wide = mel_ref[...].astype(jnp.float32)
    for f in range(FRAMES + LOOK):
        mel_t[f * rows : (f + 1) * rows, :] = mel_wide[:, f * MELS : (f + 1) * MELS]
    span = MELS
    pre = jnp.dot(
        mel_t[0 : FRAMES * rows, :].astype(jnp.bfloat16), wpre_ref[0:span, :],
        preferred_element_type=jnp.float32,
    )
    for k in range(1, LOOK + 1):
        pre = pre + jnp.dot(
            mel_t[k * rows : (k + FRAMES) * rows, :].astype(jnp.bfloat16),
            wpre_ref[k * span : (k + 1) * span, :],
            preferred_element_type=jnp.float32,
        )
    pre_act = leaky_relu(pre).astype(jnp.bfloat16)
    for j in range(UP):
        cols = slice(j * C1, (j + 1) * C1)
        part = jnp.dot(pre_act, wup_ref[C0 : 2 * C0, cols], preferred_element_type=jnp.float32)
        rest = jnp.dot(
            pre_act[: (FRAMES - 1) * rows], wup_ref[0:C0, cols], preferred_element_type=jnp.float32
        )
        x_ref[pl.ds(j * rows, rows), :] = part[0:rows]
        for t in range(1, FRAMES):
            slab = part[t * rows : (t + 1) * rows] + rest[(t - 1) * rows : t * rows]
            x_ref[pl.ds((UP * t + j) * rows, rows), :] = slab
            a_ref[pl.ds((2 * DILATIONS[0] + UP * t + j) * rows, rows), :] = leaky_relu(slab).astype(
                jnp.bfloat16
            )

    fetch(0)
    start_piece(old_ref, arrived, *IN_PIECES[2], in_send, in_recv, in_local, 2)
    head = jnp.dot(held[:, 0:C0], wup_ref[0:C0, :], preferred_element_type=jnp.float32)
    for j in range(UP):
        slab = x_ref[pl.ds(j * rows, rows), :] + head[:, j * C1 : (j + 1) * C1]
        x_ref[pl.ds(j * rows, rows), :] = slab
        a_ref[pl.ds((2 * DILATIONS[0] + j) * rows, rows), :] = leaky_relu(slab).astype(jnp.bfloat16)
    kept[:, 0:C0] = jnp.where(live, pre_act[(FRAMES - 1) * rows :], held[:, 0:C0])

    offset = C0
    steps = length * rows // CHUNK
    for section, dilation in enumerate(DILATIONS):
        if section > 0:
            fetch(section)
        a_off = offset
        for p in range(2 * dilation):
            a_ref[pl.ds(p * rows, rows), :] = held[:, offset + p * C1 : offset + (p + 1) * C1]
        offset = offset + 2 * dilation * C1
        e_off = offset
        for p in range(2):
            e_ref[pl.ds(p * rows, rows), :] = held[:, offset + p * C1 : offset + (p + 1) * C1]
        offset = offset + 2 * C1

        def fill(c, carry, dilation=dilation):
            r = pl.multiple_of(c * CHUNK, CHUNK)
            a_ref[pl.ds(pl.multiple_of(2 * dilation * rows + r, 16), CHUNK), :] = leaky_relu(
                x_ref[pl.ds(r, CHUNK), :]
            ).astype(jnp.bfloat16)
            return carry

        for p in range(2 * dilation):
            kept[:, a_off + p * C1 : a_off + (p + 1) * C1] = jnp.where(
                live,
                a_ref[pl.ds((length + p) * rows, rows), :],
                held[:, a_off + p * C1 : a_off + (p + 1) * C1],
            )
        if section == 2:
            post(2)

        def first(c, carry, dilation=dilation, section=section):
            r = pl.multiple_of(c * CHUNK, CHUNK)
            z = jnp.dot(
                a_ref[pl.ds(r, CHUNK), :], rf_ref[section, 0:C1, :],
                preferred_element_type=jnp.float32,
            )
            for k in (1, 2):
                z = z + jnp.dot(
                    a_ref[pl.ds(pl.multiple_of(r + k * dilation * rows, 16), CHUNK), :],
                    rf_ref[section, k * C1 : (k + 1) * C1, :],
                    preferred_element_type=jnp.float32,
                )
            e_ref[pl.ds(pl.multiple_of(2 * rows + r, 16), CHUNK), :] = leaky_relu(z).astype(
                jnp.bfloat16
            )
            return carry

        lax.fori_loop(0, steps, first, 0)
        for p in range(2):
            kept[:, e_off + p * C1 : e_off + (p + 1) * C1] = jnp.where(
                live,
                e_ref[pl.ds((length + p) * rows, rows), :],
                held[:, e_off + p * C1 : e_off + (p + 1) * C1],
            )
        post(section if section < 2 else 3)

        def second(c, carry, section=section):
            r = pl.multiple_of(c * CHUNK, CHUNK)
            z = x_ref[pl.ds(r, CHUNK), :]
            for k in range(3):
                z = z + jnp.dot(
                    e_ref[pl.ds(pl.multiple_of(r + k * rows, 16), CHUNK), :],
                    rs_ref[section, k * C1 : (k + 1) * C1, :],
                    preferred_element_type=jnp.float32,
                )
            x_ref[pl.ds(r, CHUNK), :] = z
            if section + 1 < len(DILATIONS):
                ahead = 2 * DILATIONS[section + 1] * rows
                a_ref[pl.ds(pl.multiple_of(ahead + r, 16), CHUNK), :] = leaky_relu(z).astype(
                    jnp.bfloat16
                )
            return carry

        if section + 1 < len(DILATIONS):
            lax.fori_loop(0, steps, second, 0)
        else:
            for c in range(steps):
                second(c, 0)
                z = x_ref[c * CHUNK : (c + 1) * CHUNK, :]
                for m in range(CHUNK // rows):
                    sample = c * CHUNK // rows + m
                    wave_ref[:, sample * C1 : (sample + 1) * C1] = jnp.where(
                        live, z[m * rows : (m + 1) * rows], 0.0
                    ).astype(jnp.bfloat16)
    for p in range(len(OUT_PIECES)):
        wait_piece(sendbuf, new_ref, *OUT_PIECES[p], out_send, out_recv, out_local, p)


def vocode_exchange(mel_rows, old_cache, new_owner, prev_owner, active, w_pre, w_up, res_first, res_second):
    n = lax.axis_size("pool")
    rows = mel_rows.shape[0]
    slot_total, width = old_cache.shape
    length = UP * FRAMES
    vmem = pl.BlockSpec(memory_space=pltpu.VMEM)
    anywhere = pl.BlockSpec(memory_space=pl.ANY)
    smem = pl.BlockSpec(memory_space=pltpu.SMEM)
    flops = 2 * rows * (FRAMES * (LOOK + 1) * MELS * C0 + FRAMES * 2 * C0 * UP * C1 + 6 * length * 3 * C1 * C1)
    return pl.pallas_call(
        fused_kernel,
        in_specs=[vmem, anywhere] + [smem] * 3 + [vmem] * 4,
        out_specs=[vmem, anywhere],
        out_shape=[
            jax.ShapeDtypeStruct((rows, length * C1), jnp.bfloat16),
            jax.ShapeDtypeStruct((slot_total, width), jnp.bfloat16),
        ],
        scratch_shapes=[
            pltpu.VMEM((slot_total, width), jnp.bfloat16),
            pltpu.VMEM((slot_total, width), jnp.bfloat16),
            pltpu.VMEM((rows, width), jnp.bfloat16),
            pltpu.VMEM((rows, width), jnp.bfloat16),
            pltpu.VMEM((length * rows, C1), jnp.float32),
            pltpu.VMEM(((length + 10) * rows, C1), jnp.bfloat16),
            pltpu.VMEM(((length + 2) * rows, C1), jnp.bfloat16),
            pltpu.VMEM(((FRAMES + LOOK) * rows, MELS), jnp.float32),
            pltpu.VMEM((rows, slot_total), jnp.bfloat16),
            pltpu.VMEM((slot_total, rows), jnp.bfloat16),
            pltpu.SemaphoreType.DMA((len(IN_PIECES), n)),
            pltpu.SemaphoreType.DMA((len(IN_PIECES), n)),
            pltpu.SemaphoreType.DMA((len(IN_PIECES),)),
            pltpu.SemaphoreType.DMA((len(OUT_PIECES), n)),
            pltpu.SemaphoreType.DMA((len(OUT_PIECES), n)),
            pltpu.SemaphoreType.DMA((len(OUT_PIECES),)),
        ],
        compiler_params=pltpu.CompilerParams(
            collective_id=0, has_side_effects=True, vmem_limit_bytes=60 * 1024 * 1024
        ),
        cost_estimate=pl.CostEstimate(flops=flops, transcendentals=0, bytes_accessed=16 * 1024 * 1024),
    )(mel_rows, old_cache, new_owner, prev_owner, active, w_pre, w_up, res_first, res_second)


def ranks_of(owners):
    members = owners.shape[1]
    same_owner = owners[:, :, None] == owners[:, None, :]
    earlier = jnp.arange(members)[None, :] < jnp.arange(members)[:, None]
    return jnp.sum((same_owner & earlier[None]).astype(jnp.int32), axis=2)


def on_device(
    mel_rows, old_cache, new_owner, prev_owner, active, w_pre, w_up, res_first, res_second
):
    return vocode_exchange(
        mel_rows, old_cache, new_owner[:, 0], prev_owner[:, 0], active, w_pre, w_up, res_first, res_second
    )


def solution(mesh):
    return jax.shard_map(
        on_device,
        mesh=mesh,
        in_specs=(
            P(("grp", "pool"), None),
            P(("grp", "pool"), None),
            P("grp", None),
            P("grp", None),
            P("grp"),
            P(),
            P(),
            P(),
            P(),
        ),
        out_specs=(P(("grp", "pool"), None), P(("grp", "pool"), None)),
        check_vma=False,
    )
```

```python
import jax
import jax.numpy as jnp
from jax import lax
from jax.experimental import pallas as pl
from jax.experimental.pallas import tpu as pltpu
from jax.sharding import PartitionSpec as P

C0 = 512
C1 = 256
MELS = 80
UP = 8
FRAMES = 18
LOOK = 6


DILATIONS = (1, 3, 5)
SLOPE = 0.1
CHUNK = 2304


def leaky_relu(values):
    return jnp.where(values >= 0, values, SLOPE * values)


MESH = pl.DeviceIdType.MESH
IN_PIECES = ((0, 1536), (1536, 3584), (3584, 6656))
OUT_PIECES = ((0, 1536), (1536, 3584), (3584, 6144), (6144, 6656))


def slot_tables(new_ref, prev_ref, act_ref, base, rows, slots, cap):
    column = lax.broadcasted_iota(jnp.int32, (rows, 1), 0)
    row = lax.broadcasted_iota(jnp.int32, (1, rows), 1)
    new_col = jnp.zeros((rows, 1), jnp.int32)
    new_row = jnp.zeros((1, rows), jnp.int32)
    prev_col = jnp.zeros((rows, 1), jnp.int32)
    prev_row = jnp.zeros((1, rows), jnp.int32)
    act_col = jnp.zeros((rows, 1), jnp.int32)
    for u in range(rows):
        new_u = new_ref[base + u]
        prev_u = prev_ref[base + u]
        new_col = jnp.where(column == u, new_u, new_col)
        new_row = jnp.where(row == u, new_u, new_row)
        prev_col = jnp.where(column == u, prev_u, prev_col)
        prev_row = jnp.where(row == u, prev_u, prev_row)
        act_col = jnp.where(column == u, act_ref[base + u], act_col)
    ids = lax.broadcasted_iota(jnp.int32, (rows, rows), 0)
    other = lax.broadcasted_iota(jnp.int32, (rows, rows), 1)
    prev_rank = jnp.sum(
        jnp.where((prev_col == prev_row) & (other < ids), 1, 0), axis=1, keepdims=True
    )
    new_rank = jnp.sum(jnp.where((new_col == new_row) & (ids < other), 1, 0), axis=0, keepdims=True)
    picking = (
        lax.broadcasted_iota(jnp.int32, (rows, slots), 1) == prev_col * cap + prev_rank
    ).astype(jnp.bfloat16)
    placing = (
        lax.broadcasted_iota(jnp.int32, (slots, rows), 0) == new_row * cap + new_rank
    ).astype(jnp.bfloat16)
    return picking, placing, act_col == 1


def fused_kernel(
    mel_ref, old_ref, new_owner_ref, prev_owner_ref, active_ref, wpre_ref, wup_ref, rf_ref, rs_ref,
    wave_ref, new_ref,
    arrived, sendbuf, held, kept, x_ref, a_ref, e_ref, mel_t, pick_ref, place_ref,
    in_send, in_recv, in_local, out_send, out_recv, out_local,
):
    n = in_send.shape[1]
    cap = old_ref.shape[0] // n
    rows = held.shape[0]
    length = UP * FRAMES
    me = lax.axis_index("pool")

    barrier = pltpu.get_barrier_semaphore()

    def greet(s, carry):
        pl.semaphore_signal(barrier, 1, device_id={"pool": lax.rem(me + s, n)}, device_id_type=MESH)
        return carry

    lax.fori_loop(1, n, greet, 0)
    pl.semaphore_wait(barrier, n - 1)

    def start_piece(src, dst, lo, hi, sends, recvs, locals_, p):
        cols = pl.ds(lo, hi - lo)
        mine = pl.ds(pl.multiple_of(me * cap, cap), cap)
        pltpu.make_async_copy(src.at[mine, cols], dst.at[mine, cols], locals_.at[p]).start()

        def body(i, carry):
            s = n - i
            peer = lax.rem(me + s, n)
            pltpu.make_async_remote_copy(
                src_ref=src.at[pl.ds(pl.multiple_of(peer * cap, cap), cap), cols],
                dst_ref=dst.at[mine, cols],
                send_sem=sends.at[p, s],
                recv_sem=recvs.at[p, s],
                device_id={"pool": peer},
                device_id_type=MESH,
            ).start()
            return carry

        lax.fori_loop(1, n, body, 0)

    def wait_piece(src, dst, lo, hi, sends, recvs, locals_, p):
        cols = pl.ds(lo, hi - lo)
        mine = pl.ds(pl.multiple_of(me * cap, cap), cap)

        def body(s, carry):
            peer = lax.rem(me + s, n)
            source = lax.rem(me + n - s, n)
            pltpu.make_async_remote_copy(
                src_ref=src.at[pl.ds(pl.multiple_of(peer * cap, cap), cap), cols],
                dst_ref=dst.at[mine, cols],
                send_sem=sends.at[p, s],
                recv_sem=recvs.at[p, s],
                device_id={"pool": peer},
                device_id_type=MESH,
            ).wait_send()
            pltpu.make_async_remote_copy(
                src_ref=src.at[pl.ds(pl.multiple_of(source * cap, cap), cap), cols],
                dst_ref=dst.at[pl.ds(pl.multiple_of(source * cap, cap), cap), cols],
                send_sem=sends.at[p, s],
                recv_sem=recvs.at[p, s],
                device_id={"pool": source},
                device_id_type=MESH,
            ).wait_recv()
            return carry

        lax.fori_loop(1, n, body, 0)
        pltpu.make_async_copy(src.at[mine, cols], dst.at[mine, cols], locals_.at[p]).wait()

    def fetch(p):
        wait_piece(old_ref, arrived, *IN_PIECES[p], in_send, in_recv, in_local, p)
        lo, hi = IN_PIECES[p]
        held[:, lo:hi] = jnp.dot(
            pick_ref[...], arrived[:, lo:hi], preferred_element_type=jnp.float32
        ).astype(jnp.bfloat16)

    def post(p):
        lo, hi = OUT_PIECES[p]
        sendbuf[:, lo:hi] = jnp.dot(
            place_ref[...], kept[:, lo:hi], preferred_element_type=jnp.float32
        ).astype(jnp.bfloat16)
        start_piece(sendbuf, new_ref, lo, hi, out_send, out_recv, out_local, p)

    start_piece(old_ref, arrived, *IN_PIECES[0], in_send, in_recv, in_local, 0)
    start_piece(old_ref, arrived, *IN_PIECES[1], in_send, in_recv, in_local, 1)

    picking, placing, live = slot_tables(
        new_owner_ref, prev_owner_ref, active_ref, me * rows, rows, old_ref.shape[0], cap
    )
    pick_ref[...] = picking
    place_ref[...] = placing
    mel_wide = mel_ref[...].astype(jnp.float32)
    for f in range(FRAMES + LOOK):
        mel_t[f * rows : (f + 1) * rows, :] = mel_wide[:, f * MELS : (f + 1) * MELS]
    span = MELS
    pre = jnp.dot(
        mel_t[0 : FRAMES * rows, :].astype(jnp.bfloat16), wpre_ref[0:span, :],
        preferred_element_type=jnp.float32,
    )
    for k in range(1, LOOK + 1):
        pre = pre + jnp.dot(
            mel_t[k * rows : (k + FRAMES) * rows, :].astype(jnp.bfloat16),
            wpre_ref[k * span : (k + 1) * span, :],
            preferred_element_type=jnp.float32,
        )
    pre_act = leaky_relu(pre).astype(jnp.bfloat16)
    for j in range(UP):
        cols = slice(j * C1, (j + 1) * C1)
        part = jnp.dot(pre_act, wup_ref[C0 : 2 * C0, cols], preferred_element_type=jnp.float32)
        rest = jnp.dot(
            pre_act[: (FRAMES - 1) * rows], wup_ref[0:C0, cols], preferred_element_type=jnp.float32
        )
        x_ref[pl.ds(j * rows, rows), :] = part[0:rows]
        for t in range(1, FRAMES):
            slab = part[t * rows : (t + 1) * rows] + rest[(t - 1) * rows : t * rows]
            x_ref[pl.ds((UP * t + j) * rows, rows), :] = slab
            a_ref[pl.ds((2 * DILATIONS[0] + UP * t + j) * rows, rows), :] = leaky_relu(slab).astype(
                jnp.bfloat16
            )

    fetch(0)
    start_piece(old_ref, arrived, *IN_PIECES[2], in_send, in_recv, in_local, 2)
    head = jnp.dot(held[:, 0:C0], wup_ref[0:C0, :], preferred_element_type=jnp.float32)
    for j in range(UP):
        slab = x_ref[pl.ds(j * rows, rows), :] + head[:, j * C1 : (j + 1) * C1]
        x_ref[pl.ds(j * rows, rows), :] = slab
        a_ref[pl.ds((2 * DILATIONS[0] + j) * rows, rows), :] = leaky_relu(slab).astype(jnp.bfloat16)
    kept[:, 0:C0] = jnp.where(live, pre_act[(FRAMES - 1) * rows :], held[:, 0:C0])

    offset = C0
    steps = length * rows // CHUNK
    for section, dilation in enumerate(DILATIONS):
        if section > 0:
            fetch(section)
        a_off = offset
        for p in range(2 * dilation):
            a_ref[pl.ds(p * rows, rows), :] = held[:, offset + p * C1 : offset + (p + 1) * C1]
        offset = offset + 2 * dilation * C1
        e_off = offset
        for p in range(2):
            e_ref[pl.ds(p * rows, rows), :] = held[:, offset + p * C1 : offset + (p + 1) * C1]
        offset = offset + 2 * C1

        def fill(c, carry, dilation=dilation):
            r = pl.multiple_of(c * CHUNK, CHUNK)
            a_ref[pl.ds(pl.multiple_of(2 * dilation * rows + r, 16), CHUNK), :] = leaky_relu(
                x_ref[pl.ds(r, CHUNK), :]
            ).astype(jnp.bfloat16)
            return carry

        for p in range(2 * dilation):
            kept[:, a_off + p * C1 : a_off + (p + 1) * C1] = jnp.where(
                live,
                a_ref[pl.ds((length + p) * rows, rows), :],
                held[:, a_off + p * C1 : a_off + (p + 1) * C1],
            )
        if section == 2:
            post(2)

        def first(c, carry, dilation=dilation, section=section):
            r = pl.multiple_of(c * CHUNK, CHUNK)
            z = jnp.dot(
                a_ref[pl.ds(r, CHUNK), :], rf_ref[section, 0:C1, :],
                preferred_element_type=jnp.float32,
            )
            for k in (1, 2):
                z = z + jnp.dot(
                    a_ref[pl.ds(pl.multiple_of(r + k * dilation * rows, 16), CHUNK), :],
                    rf_ref[section, k * C1 : (k + 1) * C1, :],
                    preferred_element_type=jnp.float32,
                )
            e_ref[pl.ds(pl.multiple_of(2 * rows + r, 16), CHUNK), :] = leaky_relu(z).astype(
                jnp.bfloat16
            )
            return carry

        lax.fori_loop(0, steps, first, 0)
        for p in range(2):
            kept[:, e_off + p * C1 : e_off + (p + 1) * C1] = jnp.where(
                live,
                e_ref[pl.ds((length + p) * rows, rows), :],
                held[:, e_off + p * C1 : e_off + (p + 1) * C1],
            )
        post(section if section < 2 else 3)

        def second(c, carry, section=section):
            r = pl.multiple_of(c * CHUNK, CHUNK)
            z = x_ref[pl.ds(r, CHUNK), :]
            for k in range(3):
                z = z + jnp.dot(
                    e_ref[pl.ds(pl.multiple_of(r + k * rows, 16), CHUNK), :],
                    rs_ref[section, k * C1 : (k + 1) * C1, :],
                    preferred_element_type=jnp.float32,
                )
            x_ref[pl.ds(r, CHUNK), :] = z
            if section + 1 < len(DILATIONS):
                ahead = 2 * DILATIONS[section + 1] * rows
                a_ref[pl.ds(pl.multiple_of(ahead + r, 16), CHUNK), :] = leaky_relu(z).astype(
                    jnp.bfloat16
                )
            return carry

        if section + 1 < len(DILATIONS):
            lax.fori_loop(0, steps, second, 0)
        else:
            for c in range(steps):
                second(c, 0)
                z = x_ref[c * CHUNK : (c + 1) * CHUNK, :]
                for m in range(CHUNK // rows):
                    sample = c * CHUNK // rows + m
                    wave_ref[:, sample * C1 : (sample + 1) * C1] = jnp.where(
                        live, z[m * rows : (m + 1) * rows], 0.0
                    ).astype(jnp.bfloat16)
    for p in range(len(OUT_PIECES)):
        wait_piece(sendbuf, new_ref, *OUT_PIECES[p], out_send, out_recv, out_local, p)


def vocode_exchange(mel_rows, old_cache, new_owner, prev_owner, active, w_pre, w_up, res_first, res_second):
    n = lax.axis_size("pool")
    rows = mel_rows.shape[0]
    slot_total, width = old_cache.shape
    length = UP * FRAMES
    vmem = pl.BlockSpec(memory_space=pltpu.VMEM)
    anywhere = pl.BlockSpec(memory_space=pl.ANY)
    smem = pl.BlockSpec(memory_space=pltpu.SMEM)
    flops = 2 * rows * (FRAMES * (LOOK + 1) * MELS * C0 + FRAMES * 2 * C0 * UP * C1 + 6 * length * 3 * C1 * C1)
    return pl.pallas_call(
        fused_kernel,
        in_specs=[vmem, anywhere] + [smem] * 3 + [vmem] * 4,
        out_specs=[vmem, anywhere],
        out_shape=[
            jax.ShapeDtypeStruct((rows, length * C1), jnp.bfloat16),
            jax.ShapeDtypeStruct((slot_total, width), jnp.bfloat16),
        ],
        scratch_shapes=[
            pltpu.VMEM((slot_total, width), jnp.bfloat16),
            pltpu.VMEM((slot_total, width), jnp.bfloat16),
            pltpu.VMEM((rows, width), jnp.bfloat16),
            pltpu.VMEM((rows, width), jnp.bfloat16),
            pltpu.VMEM((length * rows, C1), jnp.float32),
            pltpu.VMEM(((length + 10) * rows, C1), jnp.bfloat16),
            pltpu.VMEM(((length + 2) * rows, C1), jnp.bfloat16),
            pltpu.VMEM(((FRAMES + LOOK) * rows, MELS), jnp.float32),
            pltpu.VMEM((rows, slot_total), jnp.bfloat16),
            pltpu.VMEM((slot_total, rows), jnp.bfloat16),
            pltpu.SemaphoreType.DMA((len(IN_PIECES), n)),
            pltpu.SemaphoreType.DMA((len(IN_PIECES), n)),
            pltpu.SemaphoreType.DMA((len(IN_PIECES),)),
            pltpu.SemaphoreType.DMA((len(OUT_PIECES), n)),
            pltpu.SemaphoreType.DMA((len(OUT_PIECES), n)),
            pltpu.SemaphoreType.DMA((len(OUT_PIECES),)),
        ],
        compiler_params=pltpu.CompilerParams(
            collective_id=0, has_side_effects=True, vmem_limit_bytes=60 * 1024 * 1024
        ),
        cost_estimate=pl.CostEstimate(flops=flops, transcendentals=0, bytes_accessed=16 * 1024 * 1024),
    )(mel_rows, old_cache, new_owner, prev_owner, active, w_pre, w_up, res_first, res_second)


def ranks_of(owners):
    members = owners.shape[1]
    same_owner = owners[:, :, None] == owners[:, None, :]
    earlier = jnp.arange(members)[None, :] < jnp.arange(members)[:, None]
    return jnp.sum((same_owner & earlier[None]).astype(jnp.int32), axis=2)


def on_device(
    mel_rows, old_cache, new_owner, prev_owner, active, w_pre, w_up, res_first, res_second
):
    return vocode_exchange(
        mel_rows, old_cache, new_owner[:, 0], prev_owner[:, 0], active, w_pre, w_up, res_first, res_second
    )


def solution(mesh):
    return jax.shard_map(
        on_device,
        mesh=mesh,
        in_specs=(
            P(("grp", "pool"), None),
            P(("grp", "pool"), None),
            P("grp", None),
            P("grp", None),
            P("grp"),
            P(),
            P(),
            P(),
            P(),
        ),
        out_specs=(P(("grp", "pool"), None), P(("grp", "pool"), None)),
        check_vma=False,
    )
```

```python
import jax
import jax.numpy as jnp
from jax import lax
from jax.experimental import pallas as pl
from jax.experimental.pallas import tpu as pltpu
from jax.sharding import PartitionSpec as P

C0 = 512
C1 = 256
MELS = 80
UP = 8
FRAMES = 18
LOOK = 6


DILATIONS = (1, 3, 5)
SLOPE = 0.1
CHUNK = 2304


def leaky_relu(values):
    return jnp.where(values >= 0, values, SLOPE * values)


MESH = pl.DeviceIdType.MESH
IN_PIECES = ((0, 1536), (1536, 3584), (3584, 6656))
OUT_PIECES = ((0, 1536), (1536, 3584), (3584, 6144), (6144, 6656))


def slot_tables(new_ref, prev_ref, act_ref, base, rows, slots, cap):
    column = lax.broadcasted_iota(jnp.int32, (rows, 1), 0)
    row = lax.broadcasted_iota(jnp.int32, (1, rows), 1)
    new_col = jnp.zeros((rows, 1), jnp.int32)
    new_row = jnp.zeros((1, rows), jnp.int32)
    prev_col = jnp.zeros((rows, 1), jnp.int32)
    prev_row = jnp.zeros((1, rows), jnp.int32)
    act_col = jnp.zeros((rows, 1), jnp.int32)
    for u in range(rows):
        new_u = new_ref[base + u]
        prev_u = prev_ref[base + u]
        new_col = jnp.where(column == u, new_u, new_col)
        new_row = jnp.where(row == u, new_u, new_row)
        prev_col = jnp.where(column == u, prev_u, prev_col)
        prev_row = jnp.where(row == u, prev_u, prev_row)
        act_col = jnp.where(column == u, act_ref[base + u], act_col)
    ids = lax.broadcasted_iota(jnp.int32, (rows, rows), 0)
    other = lax.broadcasted_iota(jnp.int32, (rows, rows), 1)
    prev_rank = jnp.sum(
        jnp.where((prev_col == prev_row) & (other < ids), 1, 0), axis=1, keepdims=True
    )
    new_rank = jnp.sum(jnp.where((new_col == new_row) & (ids < other), 1, 0), axis=0, keepdims=True)
    picking = (
        lax.broadcasted_iota(jnp.int32, (rows, slots), 1) == prev_col * cap + prev_rank
    ).astype(jnp.bfloat16)
    placing = (
        lax.broadcasted_iota(jnp.int32, (slots, rows), 0) == new_row * cap + new_rank
    ).astype(jnp.bfloat16)
    return picking, placing, act_col == 1


def fused_kernel(
    mel_ref, old_ref, new_owner_ref, prev_owner_ref, active_ref, wpre_ref, wup_ref, rf_ref, rs_ref,
    wave_ref, new_ref,
    arrived, sendbuf, held, kept, x_ref, a_ref, e_ref, mel_t, pick_ref, place_ref,
    in_send, in_recv, in_local, out_send, out_recv, out_local,
):
    n = in_send.shape[1]
    cap = old_ref.shape[0] // n
    rows = held.shape[0]
    length = UP * FRAMES
    me = lax.axis_index("pool")

    barrier = pltpu.get_barrier_semaphore()

    def greet(s, carry):
        pl.semaphore_signal(barrier, 1, device_id={"pool": lax.rem(me + s, n)}, device_id_type=MESH)
        return carry

    lax.fori_loop(1, n, greet, 0)
    pl.semaphore_wait(barrier, n - 1)

    def start_piece(src, dst, lo, hi, sends, recvs, locals_, p):
        cols = pl.ds(lo, hi - lo)
        mine = pl.ds(pl.multiple_of(me * cap, cap), cap)
        pltpu.make_async_copy(src.at[mine, cols], dst.at[mine, cols], locals_.at[p]).start()

        def body(i, carry):
            s = n - i
            peer = lax.rem(me + s, n)
            pltpu.make_async_remote_copy(
                src_ref=src.at[pl.ds(pl.multiple_of(peer * cap, cap), cap), cols],
                dst_ref=dst.at[mine, cols],
                send_sem=sends.at[p, s],
                recv_sem=recvs.at[p, s],
                device_id={"pool": peer},
                device_id_type=MESH,
            ).start()
            return carry

        lax.fori_loop(1, n, body, 0)

    def wait_piece(src, dst, lo, hi, sends, recvs, locals_, p):
        cols = pl.ds(lo, hi - lo)
        mine = pl.ds(pl.multiple_of(me * cap, cap), cap)

        def body(s, carry):
            peer = lax.rem(me + s, n)
            source = lax.rem(me + n - s, n)
            pltpu.make_async_remote_copy(
                src_ref=src.at[pl.ds(pl.multiple_of(peer * cap, cap), cap), cols],
                dst_ref=dst.at[mine, cols],
                send_sem=sends.at[p, s],
                recv_sem=recvs.at[p, s],
                device_id={"pool": peer},
                device_id_type=MESH,
            ).wait_send()
            pltpu.make_async_remote_copy(
                src_ref=src.at[pl.ds(pl.multiple_of(source * cap, cap), cap), cols],
                dst_ref=dst.at[pl.ds(pl.multiple_of(source * cap, cap), cap), cols],
                send_sem=sends.at[p, s],
                recv_sem=recvs.at[p, s],
                device_id={"pool": source},
                device_id_type=MESH,
            ).wait_recv()
            return carry

        lax.fori_loop(1, n, body, 0)
        pltpu.make_async_copy(src.at[mine, cols], dst.at[mine, cols], locals_.at[p]).wait()

    def fetch(p):
        wait_piece(old_ref, arrived, *IN_PIECES[p], in_send, in_recv, in_local, p)
        lo, hi = IN_PIECES[p]
        held[:, lo:hi] = jnp.dot(
            pick_ref[...], arrived[:, lo:hi], preferred_element_type=jnp.float32
        ).astype(jnp.bfloat16)

    def post(p):
        lo, hi = OUT_PIECES[p]
        sendbuf[:, lo:hi] = jnp.dot(
            place_ref[...], kept[:, lo:hi], preferred_element_type=jnp.float32
        ).astype(jnp.bfloat16)
        start_piece(sendbuf, new_ref, lo, hi, out_send, out_recv, out_local, p)

    start_piece(old_ref, arrived, *IN_PIECES[0], in_send, in_recv, in_local, 0)
    start_piece(old_ref, arrived, *IN_PIECES[1], in_send, in_recv, in_local, 1)
    start_piece(old_ref, arrived, *IN_PIECES[2], in_send, in_recv, in_local, 2)

    picking, placing, live = slot_tables(
        new_owner_ref, prev_owner_ref, active_ref, me * rows, rows, old_ref.shape[0], cap
    )
    pick_ref[...] = picking
    place_ref[...] = placing
    mel_wide = mel_ref[...].astype(jnp.float32)
    for f in range(FRAMES + LOOK):
        mel_t[f * rows : (f + 1) * rows, :] = mel_wide[:, f * MELS : (f + 1) * MELS]
    span = MELS
    pre = jnp.dot(
        mel_t[0 : FRAMES * rows, :].astype(jnp.bfloat16), wpre_ref[0:span, :],
        preferred_element_type=jnp.float32,
    )
    for k in range(1, LOOK + 1):
        pre = pre + jnp.dot(
            mel_t[k * rows : (k + FRAMES) * rows, :].astype(jnp.bfloat16),
            wpre_ref[k * span : (k + 1) * span, :],
            preferred_element_type=jnp.float32,
        )
    pre_act = leaky_relu(pre).astype(jnp.bfloat16)
    for j in range(UP):
        cols = slice(j * C1, (j + 1) * C1)
        part = jnp.dot(pre_act, wup_ref[C0 : 2 * C0, cols], preferred_element_type=jnp.float32)
        rest = jnp.dot(
            pre_act[: (FRAMES - 1) * rows], wup_ref[0:C0, cols], preferred_element_type=jnp.float32
        )
        x_ref[pl.ds(j * rows, rows), :] = part[0:rows]
        for t in range(1, FRAMES):
            slab = part[t * rows : (t + 1) * rows] + rest[(t - 1) * rows : t * rows]
            x_ref[pl.ds((UP * t + j) * rows, rows), :] = slab
            a_ref[pl.ds((2 * DILATIONS[0] + UP * t + j) * rows, rows), :] = leaky_relu(slab).astype(
                jnp.bfloat16
            )

    fetch(0)
    head = jnp.dot(held[:, 0:C0], wup_ref[0:C0, :], preferred_element_type=jnp.float32)
    for j in range(UP):
        slab = x_ref[pl.ds(j * rows, rows), :] + head[:, j * C1 : (j + 1) * C1]
        x_ref[pl.ds(j * rows, rows), :] = slab
        a_ref[pl.ds((2 * DILATIONS[0] + j) * rows, rows), :] = leaky_relu(slab).astype(jnp.bfloat16)
    kept[:, 0:C0] = jnp.where(live, pre_act[(FRAMES - 1) * rows :], held[:, 0:C0])

    offset = C0
    steps = length * rows // CHUNK
    for section, dilation in enumerate(DILATIONS):
        if section > 0:
            fetch(section)
        a_off = offset
        for p in range(2 * dilation):
            a_ref[pl.ds(p * rows, rows), :] = held[:, offset + p * C1 : offset + (p + 1) * C1]
        offset = offset + 2 * dilation * C1
        e_off = offset
        for p in range(2):
            e_ref[pl.ds(p * rows, rows), :] = held[:, offset + p * C1 : offset + (p + 1) * C1]
        offset = offset + 2 * C1

        def fill(c, carry, dilation=dilation):
            r = pl.multiple_of(c * CHUNK, CHUNK)
            a_ref[pl.ds(pl.multiple_of(2 * dilation * rows + r, 16), CHUNK), :] = leaky_relu(
                x_ref[pl.ds(r, CHUNK), :]
            ).astype(jnp.bfloat16)
            return carry

        for p in range(2 * dilation):
            kept[:, a_off + p * C1 : a_off + (p + 1) * C1] = jnp.where(
                live,
                a_ref[pl.ds((length + p) * rows, rows), :],
                held[:, a_off + p * C1 : a_off + (p + 1) * C1],
            )
        if section == 2:
            post(2)

        def first(c, carry, dilation=dilation, section=section):
            r = pl.multiple_of(c * CHUNK, CHUNK)
            z = jnp.dot(
                a_ref[pl.ds(r, CHUNK), :], rf_ref[section, 0:C1, :],
                preferred_element_type=jnp.float32,
            )
            for k in (1, 2):
                z = z + jnp.dot(
                    a_ref[pl.ds(pl.multiple_of(r + k * dilation * rows, 16), CHUNK), :],
                    rf_ref[section, k * C1 : (k + 1) * C1, :],
                    preferred_element_type=jnp.float32,
                )
            e_ref[pl.ds(pl.multiple_of(2 * rows + r, 16), CHUNK), :] = leaky_relu(z).astype(
                jnp.bfloat16
            )
            return carry

        lax.fori_loop(0, steps, first, 0)
        for p in range(2):
            kept[:, e_off + p * C1 : e_off + (p + 1) * C1] = jnp.where(
                live,
                e_ref[pl.ds((length + p) * rows, rows), :],
                held[:, e_off + p * C1 : e_off + (p + 1) * C1],
            )
        post(section if section < 2 else 3)

        def second(c, carry, section=section):
            r = pl.multiple_of(c * CHUNK, CHUNK)
            z = x_ref[pl.ds(r, CHUNK), :]
            for k in range(3):
                z = z + jnp.dot(
                    e_ref[pl.ds(pl.multiple_of(r + k * rows, 16), CHUNK), :],
                    rs_ref[section, k * C1 : (k + 1) * C1, :],
                    preferred_element_type=jnp.float32,
                )
            x_ref[pl.ds(r, CHUNK), :] = z
            if section + 1 < len(DILATIONS):
                ahead = 2 * DILATIONS[section + 1] * rows
                a_ref[pl.ds(pl.multiple_of(ahead + r, 16), CHUNK), :] = leaky_relu(z).astype(
                    jnp.bfloat16
                )
            return carry

        if section + 1 < len(DILATIONS):
            lax.fori_loop(0, steps, second, 0)
        else:
            for c in range(steps):
                second(c, 0)
                z = x_ref[c * CHUNK : (c + 1) * CHUNK, :]
                for m in range(CHUNK // rows):
                    sample = c * CHUNK // rows + m
                    wave_ref[:, sample * C1 : (sample + 1) * C1] = jnp.where(
                        live, z[m * rows : (m + 1) * rows], 0.0
                    ).astype(jnp.bfloat16)
    for p in range(len(OUT_PIECES)):
        wait_piece(sendbuf, new_ref, *OUT_PIECES[p], out_send, out_recv, out_local, p)


def vocode_exchange(mel_rows, old_cache, new_owner, prev_owner, active, w_pre, w_up, res_first, res_second):
    n = lax.axis_size("pool")
    rows = mel_rows.shape[0]
    slot_total, width = old_cache.shape
    length = UP * FRAMES
    vmem = pl.BlockSpec(memory_space=pltpu.VMEM)
    anywhere = pl.BlockSpec(memory_space=pl.ANY)
    smem = pl.BlockSpec(memory_space=pltpu.SMEM)
    flops = 2 * rows * (FRAMES * (LOOK + 1) * MELS * C0 + FRAMES * 2 * C0 * UP * C1 + 6 * length * 3 * C1 * C1)
    return pl.pallas_call(
        fused_kernel,
        in_specs=[vmem, anywhere] + [smem] * 3 + [vmem] * 4,
        out_specs=[vmem, anywhere],
        out_shape=[
            jax.ShapeDtypeStruct((rows, length * C1), jnp.bfloat16),
            jax.ShapeDtypeStruct((slot_total, width), jnp.bfloat16),
        ],
        scratch_shapes=[
            pltpu.VMEM((slot_total, width), jnp.bfloat16),
            pltpu.VMEM((slot_total, width), jnp.bfloat16),
            pltpu.VMEM((rows, width), jnp.bfloat16),
            pltpu.VMEM((rows, width), jnp.bfloat16),
            pltpu.VMEM((length * rows, C1), jnp.float32),
            pltpu.VMEM(((length + 10) * rows, C1), jnp.bfloat16),
            pltpu.VMEM(((length + 2) * rows, C1), jnp.bfloat16),
            pltpu.VMEM(((FRAMES + LOOK) * rows, MELS), jnp.float32),
            pltpu.VMEM((rows, slot_total), jnp.bfloat16),
            pltpu.VMEM((slot_total, rows), jnp.bfloat16),
            pltpu.SemaphoreType.DMA((len(IN_PIECES), n)),
            pltpu.SemaphoreType.DMA((len(IN_PIECES), n)),
            pltpu.SemaphoreType.DMA((len(IN_PIECES),)),
            pltpu.SemaphoreType.DMA((len(OUT_PIECES), n)),
            pltpu.SemaphoreType.DMA((len(OUT_PIECES), n)),
            pltpu.SemaphoreType.DMA((len(OUT_PIECES),)),
        ],
        compiler_params=pltpu.CompilerParams(
            collective_id=0, has_side_effects=True, vmem_limit_bytes=60 * 1024 * 1024
        ),
        cost_estimate=pl.CostEstimate(flops=flops, transcendentals=0, bytes_accessed=16 * 1024 * 1024),
    )(mel_rows, old_cache, new_owner, prev_owner, active, w_pre, w_up, res_first, res_second)


def ranks_of(owners):
    members = owners.shape[1]
    same_owner = owners[:, :, None] == owners[:, None, :]
    earlier = jnp.arange(members)[None, :] < jnp.arange(members)[:, None]
    return jnp.sum((same_owner & earlier[None]).astype(jnp.int32), axis=2)


def on_device(
    mel_rows, old_cache, new_owner, prev_owner, active, w_pre, w_up, res_first, res_second
):
    return vocode_exchange(
        mel_rows, old_cache, new_owner[:, 0], prev_owner[:, 0], active, w_pre, w_up, res_first, res_second
    )


def solution(mesh):
    return jax.shard_map(
        on_device,
        mesh=mesh,
        in_specs=(
            P(("grp", "pool"), None),
            P(("grp", "pool"), None),
            P("grp", None),
            P("grp", None),
            P("grp"),
            P(),
            P(),
            P(),
            P(),
        ),
        out_specs=(P(("grp", "pool"), None), P(("grp", "pool"), None)),
        check_vma=False,
    )
```

```python
import jax
import jax.numpy as jnp
from jax import lax
from jax.experimental import pallas as pl
from jax.experimental.pallas import tpu as pltpu
from jax.sharding import PartitionSpec as P

C0 = 512
C1 = 256
MELS = 80
UP = 8
FRAMES = 18
LOOK = 6


DILATIONS = (1, 3, 5)
SLOPE = 0.1
CHUNK = 2304


def leaky_relu(values):
    return jnp.where(values >= 0, values, SLOPE * values)


MESH = pl.DeviceIdType.MESH
IN_PIECES = ((0, 1536), (1536, 3584), (3584, 6656))
OUT_PIECES = ((0, 1536), (1536, 3584), (3584, 6144), (6144, 6656))


def slot_tables(new_ref, prev_ref, act_ref, base, rows, slots, cap):
    column = lax.broadcasted_iota(jnp.int32, (rows, 1), 0)
    row = lax.broadcasted_iota(jnp.int32, (1, rows), 1)
    new_col = jnp.zeros((rows, 1), jnp.int32)
    new_row = jnp.zeros((1, rows), jnp.int32)
    prev_col = jnp.zeros((rows, 1), jnp.int32)
    prev_row = jnp.zeros((1, rows), jnp.int32)
    act_col = jnp.zeros((rows, 1), jnp.int32)
    for u in range(rows):
        new_u = new_ref[base + u]
        prev_u = prev_ref[base + u]
        new_col = jnp.where(column == u, new_u, new_col)
        new_row = jnp.where(row == u, new_u, new_row)
        prev_col = jnp.where(column == u, prev_u, prev_col)
        prev_row = jnp.where(row == u, prev_u, prev_row)
        act_col = jnp.where(column == u, act_ref[base + u], act_col)
    ids = lax.broadcasted_iota(jnp.int32, (rows, rows), 0)
    other = lax.broadcasted_iota(jnp.int32, (rows, rows), 1)
    prev_rank = jnp.sum(
        jnp.where((prev_col == prev_row) & (other < ids), 1, 0), axis=1, keepdims=True
    )
    new_rank = jnp.sum(jnp.where((new_col == new_row) & (ids < other), 1, 0), axis=0, keepdims=True)
    picking = (
        lax.broadcasted_iota(jnp.int32, (rows, slots), 1) == prev_col * cap + prev_rank
    ).astype(jnp.bfloat16)
    placing = (
        lax.broadcasted_iota(jnp.int32, (slots, rows), 0) == new_row * cap + new_rank
    ).astype(jnp.bfloat16)
    return picking, placing, act_col == 1


def fused_kernel(
    mel_ref, old_ref, new_owner_ref, prev_owner_ref, active_ref, wpre_hbm, wup_hbm, rf_hbm, rs_hbm,
    wave_ref, new_ref,
    arrived, sendbuf, held, kept, x_ref, a_ref, e_ref, mel_t, pick_ref, place_ref,
    wpre_ref, wup_ref, rf_ref, rs_ref, weight_sem,
    in_send, in_recv, in_local, out_send, out_recv, out_local,
):
    loads = [
        pltpu.make_async_copy(source, target, weight_sem.at[i])
        for i, (source, target) in enumerate(
            ((wpre_hbm, wpre_ref), (wup_hbm, wup_ref), (rf_hbm, rf_ref), (rs_hbm, rs_ref))
        )
    ]
    for load in loads:
        load.start()
    n = in_send.shape[1]
    cap = old_ref.shape[0] // n
    rows = held.shape[0]
    length = UP * FRAMES
    me = lax.axis_index("pool")

    barrier = pltpu.get_barrier_semaphore()

    def greet(s, carry):
        pl.semaphore_signal(barrier, 1, device_id={"pool": lax.rem(me + s, n)}, device_id_type=MESH)
        return carry

    lax.fori_loop(1, n, greet, 0)
    pl.semaphore_wait(barrier, n - 1)

    def start_piece(src, dst, lo, hi, sends, recvs, locals_, p):
        cols = pl.ds(lo, hi - lo)
        mine = pl.ds(pl.multiple_of(me * cap, cap), cap)
        pltpu.make_async_copy(src.at[mine, cols], dst.at[mine, cols], locals_.at[p]).start()

        def body(i, carry):
            s = n - i
            peer = lax.rem(me + s, n)
            pltpu.make_async_remote_copy(
                src_ref=src.at[pl.ds(pl.multiple_of(peer * cap, cap), cap), cols],
                dst_ref=dst.at[mine, cols],
                send_sem=sends.at[p, s],
                recv_sem=recvs.at[p, s],
                device_id={"pool": peer},
                device_id_type=MESH,
            ).start()
            return carry

        lax.fori_loop(1, n, body, 0)

    def wait_piece(src, dst, lo, hi, sends, recvs, locals_, p):
        cols = pl.ds(lo, hi - lo)
        mine = pl.ds(pl.multiple_of(me * cap, cap), cap)

        def body(s, carry):
            peer = lax.rem(me + s, n)
            source = lax.rem(me + n - s, n)
            pltpu.make_async_remote_copy(
                src_ref=src.at[pl.ds(pl.multiple_of(peer * cap, cap), cap), cols],
                dst_ref=dst.at[mine, cols],
                send_sem=sends.at[p, s],
                recv_sem=recvs.at[p, s],
                device_id={"pool": peer},
                device_id_type=MESH,
            ).wait_send()
            pltpu.make_async_remote_copy(
                src_ref=src.at[pl.ds(pl.multiple_of(source * cap, cap), cap), cols],
                dst_ref=dst.at[pl.ds(pl.multiple_of(source * cap, cap), cap), cols],
                send_sem=sends.at[p, s],
                recv_sem=recvs.at[p, s],
                device_id={"pool": source},
                device_id_type=MESH,
            ).wait_recv()
            return carry

        lax.fori_loop(1, n, body, 0)
        pltpu.make_async_copy(src.at[mine, cols], dst.at[mine, cols], locals_.at[p]).wait()

    def fetch(p):
        wait_piece(old_ref, arrived, *IN_PIECES[p], in_send, in_recv, in_local, p)
        lo, hi = IN_PIECES[p]
        held[:, lo:hi] = jnp.dot(
            pick_ref[...], arrived[:, lo:hi], preferred_element_type=jnp.float32
        ).astype(jnp.bfloat16)

    def post(p):
        lo, hi = OUT_PIECES[p]
        sendbuf[:, lo:hi] = jnp.dot(
            place_ref[...], kept[:, lo:hi], preferred_element_type=jnp.float32
        ).astype(jnp.bfloat16)
        start_piece(sendbuf, new_ref, lo, hi, out_send, out_recv, out_local, p)

    start_piece(old_ref, arrived, *IN_PIECES[0], in_send, in_recv, in_local, 0)
    start_piece(old_ref, arrived, *IN_PIECES[1], in_send, in_recv, in_local, 1)
    start_piece(old_ref, arrived, *IN_PIECES[2], in_send, in_recv, in_local, 2)

    picking, placing, live = slot_tables(
        new_owner_ref, prev_owner_ref, active_ref, me * rows, rows, old_ref.shape[0], cap
    )
    pick_ref[...] = picking
    place_ref[...] = placing
    mel_wide = mel_ref[...].astype(jnp.float32)
    for f in range(FRAMES + LOOK):
        mel_t[f * rows : (f + 1) * rows, :] = mel_wide[:, f * MELS : (f + 1) * MELS]
    span = MELS
    loads[0].wait()
    pre = jnp.dot(
        mel_t[0 : FRAMES * rows, :].astype(jnp.bfloat16), wpre_ref[0:span, :],
        preferred_element_type=jnp.float32,
    )
    for k in range(1, LOOK + 1):
        pre = pre + jnp.dot(
            mel_t[k * rows : (k + FRAMES) * rows, :].astype(jnp.bfloat16),
            wpre_ref[k * span : (k + 1) * span, :],
            preferred_element_type=jnp.float32,
        )
    pre_act = leaky_relu(pre).astype(jnp.bfloat16)
    loads[1].wait()
    for j in range(UP):
        cols = slice(j * C1, (j + 1) * C1)
        part = jnp.dot(pre_act, wup_ref[C0 : 2 * C0, cols], preferred_element_type=jnp.float32)
        rest = jnp.dot(
            pre_act[: (FRAMES - 1) * rows], wup_ref[0:C0, cols], preferred_element_type=jnp.float32
        )
        x_ref[pl.ds(j * rows, rows), :] = part[0:rows]
        for t in range(1, FRAMES):
            slab = part[t * rows : (t + 1) * rows] + rest[(t - 1) * rows : t * rows]
            x_ref[pl.ds((UP * t + j) * rows, rows), :] = slab
            a_ref[pl.ds((2 * DILATIONS[0] + UP * t + j) * rows, rows), :] = leaky_relu(slab).astype(
                jnp.bfloat16
            )

    fetch(0)
    head = jnp.dot(held[:, 0:C0], wup_ref[0:C0, :], preferred_element_type=jnp.float32)
    for j in range(UP):
        slab = x_ref[pl.ds(j * rows, rows), :] + head[:, j * C1 : (j + 1) * C1]
        x_ref[pl.ds(j * rows, rows), :] = slab
        a_ref[pl.ds((2 * DILATIONS[0] + j) * rows, rows), :] = leaky_relu(slab).astype(jnp.bfloat16)
    kept[:, 0:C0] = jnp.where(live, pre_act[(FRAMES - 1) * rows :], held[:, 0:C0])

    loads[2].wait()
    loads[3].wait()
    offset = C0
    steps = length * rows // CHUNK
    for section, dilation in enumerate(DILATIONS):
        if section > 0:
            fetch(section)
        a_off = offset
        for p in range(2 * dilation):
            a_ref[pl.ds(p * rows, rows), :] = held[:, offset + p * C1 : offset + (p + 1) * C1]
        offset = offset + 2 * dilation * C1
        e_off = offset
        for p in range(2):
            e_ref[pl.ds(p * rows, rows), :] = held[:, offset + p * C1 : offset + (p + 1) * C1]
        offset = offset + 2 * C1

        def fill(c, carry, dilation=dilation):
            r = pl.multiple_of(c * CHUNK, CHUNK)
            a_ref[pl.ds(pl.multiple_of(2 * dilation * rows + r, 16), CHUNK), :] = leaky_relu(
                x_ref[pl.ds(r, CHUNK), :]
            ).astype(jnp.bfloat16)
            return carry

        for p in range(2 * dilation):
            kept[:, a_off + p * C1 : a_off + (p + 1) * C1] = jnp.where(
                live,
                a_ref[pl.ds((length + p) * rows, rows), :],
                held[:, a_off + p * C1 : a_off + (p + 1) * C1],
            )
        if section == 2:
            post(2)

        def first(c, carry, dilation=dilation, section=section):
            r = pl.multiple_of(c * CHUNK, CHUNK)
            z = jnp.dot(
                a_ref[pl.ds(r, CHUNK), :], rf_ref[section, 0:C1, :],
                preferred_element_type=jnp.float32,
            )
            for k in (1, 2):
                z = z + jnp.dot(
                    a_ref[pl.ds(pl.multiple_of(r + k * dilation * rows, 16), CHUNK), :],
                    rf_ref[section, k * C1 : (k + 1) * C1, :],
                    preferred_element_type=jnp.float32,
                )
            e_ref[pl.ds(pl.multiple_of(2 * rows + r, 16), CHUNK), :] = leaky_relu(z).astype(
                jnp.bfloat16
            )
            return carry

        lax.fori_loop(0, steps, first, 0)
        for p in range(2):
            kept[:, e_off + p * C1 : e_off + (p + 1) * C1] = jnp.where(
                live,
                e_ref[pl.ds((length + p) * rows, rows), :],
                held[:, e_off + p * C1 : e_off + (p + 1) * C1],
            )
        post(section if section < 2 else 3)

        def second(c, carry, section=section):
            r = pl.multiple_of(c * CHUNK, CHUNK)
            z = x_ref[pl.ds(r, CHUNK), :]
            for k in range(3):
                z = z + jnp.dot(
                    e_ref[pl.ds(pl.multiple_of(r + k * rows, 16), CHUNK), :],
                    rs_ref[section, k * C1 : (k + 1) * C1, :],
                    preferred_element_type=jnp.float32,
                )
            x_ref[pl.ds(r, CHUNK), :] = z
            if section + 1 < len(DILATIONS):
                ahead = 2 * DILATIONS[section + 1] * rows
                a_ref[pl.ds(pl.multiple_of(ahead + r, 16), CHUNK), :] = leaky_relu(z).astype(
                    jnp.bfloat16
                )
            return carry

        if section + 1 < len(DILATIONS):
            lax.fori_loop(0, steps, second, 0)
        else:
            for c in range(steps):
                second(c, 0)
                z = x_ref[c * CHUNK : (c + 1) * CHUNK, :]
                for m in range(CHUNK // rows):
                    sample = c * CHUNK // rows + m
                    wave_ref[:, sample * C1 : (sample + 1) * C1] = jnp.where(
                        live, z[m * rows : (m + 1) * rows], 0.0
                    ).astype(jnp.bfloat16)
    for p in range(len(OUT_PIECES)):
        wait_piece(sendbuf, new_ref, *OUT_PIECES[p], out_send, out_recv, out_local, p)


def vocode_exchange(mel_rows, old_cache, new_owner, prev_owner, active, w_pre, w_up, res_first, res_second):
    n = lax.axis_size("pool")
    rows = mel_rows.shape[0]
    slot_total, width = old_cache.shape
    length = UP * FRAMES
    vmem = pl.BlockSpec(memory_space=pltpu.VMEM)
    anywhere = pl.BlockSpec(memory_space=pl.ANY)
    smem = pl.BlockSpec(memory_space=pltpu.SMEM)
    flops = 2 * rows * (FRAMES * (LOOK + 1) * MELS * C0 + FRAMES * 2 * C0 * UP * C1 + 6 * length * 3 * C1 * C1)
    return pl.pallas_call(
        fused_kernel,
        in_specs=[vmem, anywhere] + [smem] * 3 + [anywhere] * 4,
        out_specs=[vmem, anywhere],
        out_shape=[
            jax.ShapeDtypeStruct((rows, length * C1), jnp.bfloat16),
            jax.ShapeDtypeStruct((slot_total, width), jnp.bfloat16),
        ],
        scratch_shapes=[
            pltpu.VMEM((slot_total, width), jnp.bfloat16),
            pltpu.VMEM((slot_total, width), jnp.bfloat16),
            pltpu.VMEM((rows, width), jnp.bfloat16),
            pltpu.VMEM((rows, width), jnp.bfloat16),
            pltpu.VMEM((length * rows, C1), jnp.float32),
            pltpu.VMEM(((length + 10) * rows, C1), jnp.bfloat16),
            pltpu.VMEM(((length + 2) * rows, C1), jnp.bfloat16),
            pltpu.VMEM(((FRAMES + LOOK) * rows, MELS), jnp.float32),
            pltpu.VMEM((rows, slot_total), jnp.bfloat16),
            pltpu.VMEM((slot_total, rows), jnp.bfloat16),
            pltpu.VMEM(w_pre.shape, w_pre.dtype),
            pltpu.VMEM(w_up.shape, w_up.dtype),
            pltpu.VMEM(res_first.shape, res_first.dtype),
            pltpu.VMEM(res_second.shape, res_second.dtype),
            pltpu.SemaphoreType.DMA((4,)),
            pltpu.SemaphoreType.DMA((len(IN_PIECES), n)),
            pltpu.SemaphoreType.DMA((len(IN_PIECES), n)),
            pltpu.SemaphoreType.DMA((len(IN_PIECES),)),
            pltpu.SemaphoreType.DMA((len(OUT_PIECES), n)),
            pltpu.SemaphoreType.DMA((len(OUT_PIECES), n)),
            pltpu.SemaphoreType.DMA((len(OUT_PIECES),)),
        ],
        compiler_params=pltpu.CompilerParams(
            collective_id=0, has_side_effects=True, vmem_limit_bytes=60 * 1024 * 1024
        ),
        cost_estimate=pl.CostEstimate(flops=flops, transcendentals=0, bytes_accessed=16 * 1024 * 1024),
    )(mel_rows, old_cache, new_owner, prev_owner, active, w_pre, w_up, res_first, res_second)


def ranks_of(owners):
    members = owners.shape[1]
    same_owner = owners[:, :, None] == owners[:, None, :]
    earlier = jnp.arange(members)[None, :] < jnp.arange(members)[:, None]
    return jnp.sum((same_owner & earlier[None]).astype(jnp.int32), axis=2)


def on_device(
    mel_rows, old_cache, new_owner, prev_owner, active, w_pre, w_up, res_first, res_second
):
    return vocode_exchange(
        mel_rows, old_cache, new_owner[:, 0], prev_owner[:, 0], active, w_pre, w_up, res_first, res_second
    )


def solution(mesh):
    return jax.shard_map(
        on_device,
        mesh=mesh,
        in_specs=(
            P(("grp", "pool"), None),
            P(("grp", "pool"), None),
            P("grp", None),
            P("grp", None),
            P("grp"),
            P(),
            P(),
            P(),
            P(),
        ),
        out_specs=(P(("grp", "pool"), None), P(("grp", "pool"), None)),
        check_vma=False,
    )
```

```python
import jax
import jax.numpy as jnp
from jax import lax
from jax.experimental import pallas as pl
from jax.experimental.pallas import tpu as pltpu
from jax.sharding import PartitionSpec as P

C0 = 512
C1 = 256
MELS = 80
UP = 8
FRAMES = 18
LOOK = 6


DILATIONS = (1, 3, 5)
SLOPE = 0.1
CHUNK = 2304


def leaky_relu(values):
    return jnp.where(values >= 0, values, SLOPE * values)


MESH = pl.DeviceIdType.MESH
IN_PIECES = ((0, 1536), (1536, 3584), (3584, 6656))
OUT_PIECES = ((0, 1536), (1536, 3584), (3584, 6144), (6144, 6656))


def slot_tables(new_ref, prev_ref, act_ref, base, rows, slots, cap):
    column = lax.broadcasted_iota(jnp.int32, (rows, 1), 0)
    row = lax.broadcasted_iota(jnp.int32, (1, rows), 1)
    new_col = jnp.zeros((rows, 1), jnp.int32)
    new_row = jnp.zeros((1, rows), jnp.int32)
    prev_col = jnp.zeros((rows, 1), jnp.int32)
    prev_row = jnp.zeros((1, rows), jnp.int32)
    act_col = jnp.zeros((rows, 1), jnp.int32)
    for u in range(rows):
        new_u = new_ref[base + u]
        prev_u = prev_ref[base + u]
        new_col = jnp.where(column == u, new_u, new_col)
        new_row = jnp.where(row == u, new_u, new_row)
        prev_col = jnp.where(column == u, prev_u, prev_col)
        prev_row = jnp.where(row == u, prev_u, prev_row)
        act_col = jnp.where(column == u, act_ref[base + u], act_col)
    ids = lax.broadcasted_iota(jnp.int32, (rows, rows), 0)
    other = lax.broadcasted_iota(jnp.int32, (rows, rows), 1)
    prev_rank = jnp.sum(
        jnp.where((prev_col == prev_row) & (other < ids), 1, 0), axis=1, keepdims=True
    )
    new_rank = jnp.sum(jnp.where((new_col == new_row) & (ids < other), 1, 0), axis=0, keepdims=True)
    picking = (
        lax.broadcasted_iota(jnp.int32, (rows, slots), 1) == prev_col * cap + prev_rank
    ).astype(jnp.bfloat16)
    placing = (
        lax.broadcasted_iota(jnp.int32, (slots, rows), 0) == new_row * cap + new_rank
    ).astype(jnp.bfloat16)
    return picking, placing, act_col == 1


def fused_kernel(
    mel_ref, old_ref, new_owner_ref, prev_owner_ref, active_ref, wpre_hbm, wup_hbm, rf_hbm, rs_hbm,
    wave_hbm, new_ref,
    arrived, sendbuf, held, kept, x_ref, a_ref, e_ref, mel_t, pick_ref, place_ref,
    wpre_ref, wup_ref, rf_ref, rs_ref, weight_sem, wave_v, wave_sem,
    in_send, in_recv, in_local, out_send, out_recv, out_local,
):
    loads = [
        pltpu.make_async_copy(source, target, weight_sem.at[i])
        for i, (source, target) in enumerate(
            ((wpre_hbm, wpre_ref), (wup_hbm, wup_ref), (rf_hbm, rf_ref), (rs_hbm, rs_ref))
        )
    ]
    for load in loads:
        load.start()
    n = in_send.shape[1]
    cap = old_ref.shape[0] // n
    rows = held.shape[0]
    length = UP * FRAMES
    me = lax.axis_index("pool")

    barrier = pltpu.get_barrier_semaphore()

    def greet(s, carry):
        pl.semaphore_signal(barrier, 1, device_id={"pool": lax.rem(me + s, n)}, device_id_type=MESH)
        return carry

    lax.fori_loop(1, n, greet, 0)
    pl.semaphore_wait(barrier, n - 1)

    def start_piece(src, dst, lo, hi, sends, recvs, locals_, p):
        cols = pl.ds(lo, hi - lo)
        mine = pl.ds(pl.multiple_of(me * cap, cap), cap)
        pltpu.make_async_copy(src.at[mine, cols], dst.at[mine, cols], locals_.at[p]).start()

        def body(i, carry):
            s = n - i
            peer = lax.rem(me + s, n)
            pltpu.make_async_remote_copy(
                src_ref=src.at[pl.ds(pl.multiple_of(peer * cap, cap), cap), cols],
                dst_ref=dst.at[mine, cols],
                send_sem=sends.at[p, s],
                recv_sem=recvs.at[p, s],
                device_id={"pool": peer},
                device_id_type=MESH,
            ).start()
            return carry

        lax.fori_loop(1, n, body, 0)

    def wait_piece(src, dst, lo, hi, sends, recvs, locals_, p):
        cols = pl.ds(lo, hi - lo)
        mine = pl.ds(pl.multiple_of(me * cap, cap), cap)

        def body(s, carry):
            peer = lax.rem(me + s, n)
            source = lax.rem(me + n - s, n)
            pltpu.make_async_remote_copy(
                src_ref=src.at[pl.ds(pl.multiple_of(peer * cap, cap), cap), cols],
                dst_ref=dst.at[mine, cols],
                send_sem=sends.at[p, s],
                recv_sem=recvs.at[p, s],
                device_id={"pool": peer},
                device_id_type=MESH,
            ).wait_send()
            pltpu.make_async_remote_copy(
                src_ref=src.at[pl.ds(pl.multiple_of(source * cap, cap), cap), cols],
                dst_ref=dst.at[pl.ds(pl.multiple_of(source * cap, cap), cap), cols],
                send_sem=sends.at[p, s],
                recv_sem=recvs.at[p, s],
                device_id={"pool": source},
                device_id_type=MESH,
            ).wait_recv()
            return carry

        lax.fori_loop(1, n, body, 0)
        pltpu.make_async_copy(src.at[mine, cols], dst.at[mine, cols], locals_.at[p]).wait()

    def fetch(p):
        wait_piece(old_ref, arrived, *IN_PIECES[p], in_send, in_recv, in_local, p)
        lo, hi = IN_PIECES[p]
        held[:, lo:hi] = jnp.dot(
            pick_ref[...], arrived[:, lo:hi], preferred_element_type=jnp.float32
        ).astype(jnp.bfloat16)

    def post(p):
        lo, hi = OUT_PIECES[p]
        sendbuf[:, lo:hi] = jnp.dot(
            place_ref[...], kept[:, lo:hi], preferred_element_type=jnp.float32
        ).astype(jnp.bfloat16)
        start_piece(sendbuf, new_ref, lo, hi, out_send, out_recv, out_local, p)

    start_piece(old_ref, arrived, *IN_PIECES[0], in_send, in_recv, in_local, 0)
    start_piece(old_ref, arrived, *IN_PIECES[1], in_send, in_recv, in_local, 1)
    start_piece(old_ref, arrived, *IN_PIECES[2], in_send, in_recv, in_local, 2)

    picking, placing, live = slot_tables(
        new_owner_ref, prev_owner_ref, active_ref, me * rows, rows, old_ref.shape[0], cap
    )
    pick_ref[...] = picking
    place_ref[...] = placing
    mel_wide = mel_ref[...].astype(jnp.float32)
    for f in range(FRAMES + LOOK):
        mel_t[f * rows : (f + 1) * rows, :] = mel_wide[:, f * MELS : (f + 1) * MELS]
    span = MELS
    loads[0].wait()
    pre = jnp.dot(
        mel_t[0 : FRAMES * rows, :].astype(jnp.bfloat16), wpre_ref[0:span, :],
        preferred_element_type=jnp.float32,
    )
    for k in range(1, LOOK + 1):
        pre = pre + jnp.dot(
            mel_t[k * rows : (k + FRAMES) * rows, :].astype(jnp.bfloat16),
            wpre_ref[k * span : (k + 1) * span, :],
            preferred_element_type=jnp.float32,
        )
    pre_act = leaky_relu(pre).astype(jnp.bfloat16)
    loads[1].wait()
    for j in range(UP):
        cols = slice(j * C1, (j + 1) * C1)
        part = jnp.dot(pre_act, wup_ref[C0 : 2 * C0, cols], preferred_element_type=jnp.float32)
        rest = jnp.dot(
            pre_act[: (FRAMES - 1) * rows], wup_ref[0:C0, cols], preferred_element_type=jnp.float32
        )
        x_ref[pl.ds(j * rows, rows), :] = part[0:rows]
        for t in range(1, FRAMES):
            slab = part[t * rows : (t + 1) * rows] + rest[(t - 1) * rows : t * rows]
            x_ref[pl.ds((UP * t + j) * rows, rows), :] = slab
            a_ref[pl.ds((2 * DILATIONS[0] + UP * t + j) * rows, rows), :] = leaky_relu(slab).astype(
                jnp.bfloat16
            )

    fetch(0)
    head = jnp.dot(held[:, 0:C0], wup_ref[0:C0, :], preferred_element_type=jnp.float32)
    for j in range(UP):
        slab = x_ref[pl.ds(j * rows, rows), :] + head[:, j * C1 : (j + 1) * C1]
        x_ref[pl.ds(j * rows, rows), :] = slab
        a_ref[pl.ds((2 * DILATIONS[0] + j) * rows, rows), :] = leaky_relu(slab).astype(jnp.bfloat16)
    kept[:, 0:C0] = jnp.where(live, pre_act[(FRAMES - 1) * rows :], held[:, 0:C0])

    loads[2].wait()
    loads[3].wait()
    offset = C0
    steps = length * rows // CHUNK
    stores = []
    for section, dilation in enumerate(DILATIONS):
        if section > 0:
            fetch(section)
        a_off = offset
        for p in range(2 * dilation):
            a_ref[pl.ds(p * rows, rows), :] = held[:, offset + p * C1 : offset + (p + 1) * C1]
        offset = offset + 2 * dilation * C1
        e_off = offset
        for p in range(2):
            e_ref[pl.ds(p * rows, rows), :] = held[:, offset + p * C1 : offset + (p + 1) * C1]
        offset = offset + 2 * C1

        def fill(c, carry, dilation=dilation):
            r = pl.multiple_of(c * CHUNK, CHUNK)
            a_ref[pl.ds(pl.multiple_of(2 * dilation * rows + r, 16), CHUNK), :] = leaky_relu(
                x_ref[pl.ds(r, CHUNK), :]
            ).astype(jnp.bfloat16)
            return carry

        for p in range(2 * dilation):
            kept[:, a_off + p * C1 : a_off + (p + 1) * C1] = jnp.where(
                live,
                a_ref[pl.ds((length + p) * rows, rows), :],
                held[:, a_off + p * C1 : a_off + (p + 1) * C1],
            )
        if section == 2:
            post(2)

        def first(c, carry, dilation=dilation, section=section):
            r = pl.multiple_of(c * CHUNK, CHUNK)
            z = jnp.dot(
                a_ref[pl.ds(r, CHUNK), :], rf_ref[section, 0:C1, :],
                preferred_element_type=jnp.float32,
            )
            for k in (1, 2):
                z = z + jnp.dot(
                    a_ref[pl.ds(pl.multiple_of(r + k * dilation * rows, 16), CHUNK), :],
                    rf_ref[section, k * C1 : (k + 1) * C1, :],
                    preferred_element_type=jnp.float32,
                )
            e_ref[pl.ds(pl.multiple_of(2 * rows + r, 16), CHUNK), :] = leaky_relu(z).astype(
                jnp.bfloat16
            )
            return carry

        lax.fori_loop(0, steps, first, 0)
        for p in range(2):
            kept[:, e_off + p * C1 : e_off + (p + 1) * C1] = jnp.where(
                live,
                e_ref[pl.ds((length + p) * rows, rows), :],
                held[:, e_off + p * C1 : e_off + (p + 1) * C1],
            )
        post(section if section < 2 else 3)

        def second(c, carry, section=section):
            r = pl.multiple_of(c * CHUNK, CHUNK)
            z = x_ref[pl.ds(r, CHUNK), :]
            for k in range(3):
                z = z + jnp.dot(
                    e_ref[pl.ds(pl.multiple_of(r + k * rows, 16), CHUNK), :],
                    rs_ref[section, k * C1 : (k + 1) * C1, :],
                    preferred_element_type=jnp.float32,
                )
            x_ref[pl.ds(r, CHUNK), :] = z
            if section + 1 < len(DILATIONS):
                ahead = 2 * DILATIONS[section + 1] * rows
                a_ref[pl.ds(pl.multiple_of(ahead + r, 16), CHUNK), :] = leaky_relu(z).astype(
                    jnp.bfloat16
                )
            return carry

        if section + 1 < len(DILATIONS):
            lax.fori_loop(0, steps, second, 0)
        else:
            for c in range(steps):
                second(c, 0)
                z = x_ref[c * CHUNK : (c + 1) * CHUNK, :]
                for m in range(CHUNK // rows):
                    sample = c * CHUNK // rows + m
                    wave_v[:, sample * C1 : (sample + 1) * C1] = jnp.where(
                        live, z[m * rows : (m + 1) * rows], 0.0
                    ).astype(jnp.bfloat16)
                span_cols = pl.ds(c * CHUNK // rows * C1, CHUNK // rows * C1)
                stores.append(
                    pltpu.make_async_copy(
                        wave_v.at[:, span_cols], wave_hbm.at[:, span_cols], wave_sem.at[c]
                    )
                )
                stores[-1].start()
    for p in range(len(OUT_PIECES)):
        wait_piece(sendbuf, new_ref, *OUT_PIECES[p], out_send, out_recv, out_local, p)
    for store in stores:
        store.wait()


def vocode_exchange(mel_rows, old_cache, new_owner, prev_owner, active, w_pre, w_up, res_first, res_second):
    n = lax.axis_size("pool")
    rows = mel_rows.shape[0]
    slot_total, width = old_cache.shape
    length = UP * FRAMES
    vmem = pl.BlockSpec(memory_space=pltpu.VMEM)
    anywhere = pl.BlockSpec(memory_space=pl.ANY)
    smem = pl.BlockSpec(memory_space=pltpu.SMEM)
    flops = 2 * rows * (FRAMES * (LOOK + 1) * MELS * C0 + FRAMES * 2 * C0 * UP * C1 + 6 * length * 3 * C1 * C1)
    return pl.pallas_call(
        fused_kernel,
        in_specs=[vmem, anywhere] + [smem] * 3 + [anywhere] * 4,
        out_specs=[anywhere, anywhere],
        out_shape=[
            jax.ShapeDtypeStruct((rows, length * C1), jnp.bfloat16),
            jax.ShapeDtypeStruct((slot_total, width), jnp.bfloat16),
        ],
        scratch_shapes=[
            pltpu.VMEM((slot_total, width), jnp.bfloat16),
            pltpu.VMEM((slot_total, width), jnp.bfloat16),
            pltpu.VMEM((rows, width), jnp.bfloat16),
            pltpu.VMEM((rows, width), jnp.bfloat16),
            pltpu.VMEM((length * rows, C1), jnp.float32),
            pltpu.VMEM(((length + 10) * rows, C1), jnp.bfloat16),
            pltpu.VMEM(((length + 2) * rows, C1), jnp.bfloat16),
            pltpu.VMEM(((FRAMES + LOOK) * rows, MELS), jnp.float32),
            pltpu.VMEM((rows, slot_total), jnp.bfloat16),
            pltpu.VMEM((slot_total, rows), jnp.bfloat16),
            pltpu.VMEM(w_pre.shape, w_pre.dtype),
            pltpu.VMEM(w_up.shape, w_up.dtype),
            pltpu.VMEM(res_first.shape, res_first.dtype),
            pltpu.VMEM(res_second.shape, res_second.dtype),
            pltpu.SemaphoreType.DMA((4,)),
            pltpu.VMEM((rows, length * C1), jnp.bfloat16),
            pltpu.SemaphoreType.DMA((length * rows // CHUNK,)),
            pltpu.SemaphoreType.DMA((len(IN_PIECES), n)),
            pltpu.SemaphoreType.DMA((len(IN_PIECES), n)),
            pltpu.SemaphoreType.DMA((len(IN_PIECES),)),
            pltpu.SemaphoreType.DMA((len(OUT_PIECES), n)),
            pltpu.SemaphoreType.DMA((len(OUT_PIECES), n)),
            pltpu.SemaphoreType.DMA((len(OUT_PIECES),)),
        ],
        compiler_params=pltpu.CompilerParams(
            collective_id=0, has_side_effects=True, vmem_limit_bytes=60 * 1024 * 1024
        ),
        cost_estimate=pl.CostEstimate(flops=flops, transcendentals=0, bytes_accessed=16 * 1024 * 1024),
    )(mel_rows, old_cache, new_owner, prev_owner, active, w_pre, w_up, res_first, res_second)


def ranks_of(owners):
    members = owners.shape[1]
    same_owner = owners[:, :, None] == owners[:, None, :]
    earlier = jnp.arange(members)[None, :] < jnp.arange(members)[:, None]
    return jnp.sum((same_owner & earlier[None]).astype(jnp.int32), axis=2)


def on_device(
    mel_rows, old_cache, new_owner, prev_owner, active, w_pre, w_up, res_first, res_second
):
    return vocode_exchange(
        mel_rows, old_cache, new_owner[:, 0], prev_owner[:, 0], active, w_pre, w_up, res_first, res_second
    )


def solution(mesh):
    return jax.shard_map(
        on_device,
        mesh=mesh,
        in_specs=(
            P(("grp", "pool"), None),
            P(("grp", "pool"), None),
            P("grp", None),
            P("grp", None),
            P("grp"),
            P(),
            P(),
            P(),
            P(),
        ),
        out_specs=(P(("grp", "pool"), None), P(("grp", "pool"), None)),
        check_vma=False,
    )
```
